512 devices in a mesh: gx: 32 (over z_lo, y), gy: 16 (over z_hi, x, core).
Axes of the slice: x: 4, y: 4, z: 16 (z_hi: 2, z_lo: 8; z = z_hi * 8 + z_lo), core: 2. Of those that a mesh axis runs over, the one named last changes fastest.
Arguments:
- vectors: float32 [8, 3, 4, 256, 2048], P(None, None, None, 'gx', 'gy'), may hold values from -2000 to 2000, as said below
- background: float32 [3, 4, 256, 2048], P(None, None, 'gx', 'gy'), may hold values from -1 to 1
- obs_site: int32 [2097152], P(('gx', 'gy')), may hold values from 0 to 12287
- obs_offset: float32 [2, 2097152], P(None, ('gx', 'gy')), may hold values from -1 to 1
- obs_error: float32 [2097152], P(('gx', 'gy')), may hold values from 0.5 to 4
Outputs:
- analysis: float32 [8, 3, 4, 256, 2048], P(None, None, None, 'gx', 'gy')
- obs_perturb: float32 [8, 2097152], P(None, ('gx', 'gy'))
The draws below stay inside these ranges and needn't reach their ends.
Inputs may be any that keep to these rules, and one draw needn't show every extreme that they name: Drawn with scales that vary over vectors, variables, levels and cells. `obs_site`: observation n lies in the tile of device n // 4096; its site is ((variable * 4 + level) * 8 + row) * 128 + column, with row and column local to that tile.
All inputs are finite; a program needn't handle non-finite values.
Results may differ from the reference program's by a relative error of at most 0.000092.
Values sent between devices are 32-bit elements; how exact they have to be, the bound alone decides.
No kernel may reach another device: no remote copies, remote signals or barrier semaphores. Data moves between devices by JAX's collectives and lax.ppermute only.
A program may use at most 192 MiB of HBM per device.

```python
import math
import jax
import jax.numpy as jnp
from jax import lax

K = 8
L = 4
CX = 8
CY = 128
OBS_DEV = 4096
NX = 256
NY = 2048
NOBS = 2097152
N_GY = 16


def draw_vectors(key, part):
    keys = jax.random.split(key, 4)
    cell_shape = (3, L, NX, NY)
    common = jnp.clip(jax.random.normal(keys[0], cell_shape, jnp.float32), -4.0, 4.0)
    own_part = jnp.clip(jax.random.normal(keys[1], (K,) + cell_shape, jnp.float32), -4.0, 4.0)
    common_weight = 0.6
    cell_range = 2.3
    field_scale = jnp.exp(jax.random.uniform(keys[2], (K, 3, L, 1, 1), jnp.float32, 0.0, 2.3))
    cell_scale = jnp.exp(jax.random.uniform(keys[3], (1, 1, 1, NX, NY), jnp.float32, 0.0, cell_range))
    ramp = (1.0 + 2.0 * jnp.arange(NX, dtype=jnp.float32) / NX).reshape(NX, 1)
    return (common_weight * common + own_part) * field_scale * cell_scale * ramp


def touch_ends(drawn, key, least, high):
    index_at = [jax.random.randint(jax.random.fold_in(key, axis), (), 0, length) for axis, length in enumerate(drawn.shape)]
    widest = drawn.shape.index(max(drawn.shape))
    next_to = index_at[:widest] + [(index_at[widest] + 1) % drawn.shape[widest]] + index_at[widest + 1:]
    return drawn.at[tuple(index_at)].set(least).at[tuple(next_to)].set(high)


def level_of(stream_key, extent, cuts, least, high):
    def one(position, blocks):
        steps = jax.random.uniform(jax.random.fold_in(jax.random.fold_in(stream_key, 6), position), (blocks,), jnp.float32, least / len(cuts), high / len(cuts))
        return jnp.repeat(jnp.exp(steps), extent[position] // blocks).reshape((-1,) + (1,) * (len(extent) - position - 1))

    factor_of = one(*cuts[0])
    for cut in cuts[1:]:
        factor_of = factor_of * one(*cut)
    return factor_of


def setup_inputs(seed: int = 0) -> dict:
    splits = jax.random.split(jax.random.key(seed), 6)
    vectors = draw_vectors(jax.random.fold_in(splits[5], 71), 0)
    background = jnp.clip(jax.random.uniform(splits[1], (3, L, NX, NY), jnp.float32, -1.0, 1.0) * level_of(splits[1], (3, L, NX, NY), ((2, 32), (3, 16)), -0.4, 0.0), -1.0, 1.0)
    obs_site = touch_ends(jax.random.randint(splits[2], (NOBS,), 0, 3 * L * CX * CY), jax.random.fold_in(splits[2], 1), 0, (3 * L * CX * CY) - 1).astype(jnp.int32)
    obs_offset = jnp.clip(jax.random.uniform(splits[3], (2, NOBS), jnp.float32, -1.0, 1.0) * level_of(splits[3], (2, NOBS), ((1, 512),), -0.4, 0.0), -1.0, 1.0)
    obs_error = jnp.clip(jnp.exp(math.log(4.0) - 2.0794415 * jax.random.uniform(splits[4], (NOBS,), jnp.float32) ** level_of(splits[4], (NOBS,), ((0, 512),), -0.2, 0.2)), 0.5, 4.0)
    return {"vectors": vectors, "background": background, "obs_site": obs_site, "obs_offset": obs_offset, "obs_error": obs_error}


step_size = 0.35
highest = lax.Precision.HIGHEST

def along_x(field):
    return 0.5 * (jnp.roll(field, -1, -2) - jnp.roll(field, 1, -2))

def along_y(field):
    return 0.5 * (jnp.roll(field, -1, -1) - jnp.roll(field, 1, -1))

def tendency(state, background):
    wind_x, wind_y, vort_abs = (background[0], background[1], background[2])
    east_part, north_part, height = (state[0], state[1], state[2])

    def advect(field):
        return wind_x * along_x(field) + wind_y * along_y(field)
    tend_east = -advect(east_part) - along_x(height) + vort_abs * north_part
    tend_north = -advect(north_part) - along_y(height) - vort_abs * east_part
    tend_height = -advect(height) - (along_x(east_part) + along_y(north_part))
    return jnp.stack([tend_east, tend_north, tend_height], axis=0)

def runge_kutta(state, background):
    section_one = state + step_size * tendency(state, background)
    section_two = 0.75 * state + 0.25 * (section_one + step_size * tendency(section_one, background))
    return state / 3.0 + 2.0 / 3.0 * (section_two + step_size * tendency(section_two, background))

def reference(vectors, background, obs_site, obs_offset, obs_error):
    bred = lax.map(lambda single: runge_kutta(single, background), vectors)
    flattened = bred.reshape(K, -1)
    cells_all = float(3 * L * NX * NY)
    gram = jnp.dot(flattened.astype(jnp.float32), flattened.T.astype(jnp.float32), precision=highest, preferred_element_type=jnp.float32) / cells_all
    count_index = jnp.arange(NOBS, dtype=jnp.int32)
    device = count_index // OBS_DEV
    plane_index = obs_site // (CX * CY)
    cell_index = obs_site % (CX * CY)
    row_index = device // N_GY * CX + cell_index // CY
    col_index = device % N_GY * CY + cell_index % CY
    shift_x = obs_offset[0]
    shift_y = obs_offset[1]
    weights_x = (jnp.maximum(-shift_x, 0.0), 1.0 - jnp.abs(shift_x), jnp.maximum(shift_x, 0.0))
    weights_y = (jnp.maximum(-shift_y, 0.0), 1.0 - jnp.abs(shift_y), jnp.maximum(shift_y, 0.0))
    projected = jnp.zeros((K, NOBS), jnp.float32)
    for step_x in (-1, 0, 1):
        for step_y in (-1, 0, 1):
            index = (plane_index * NX + (row_index + step_x) % NX) * NY + (col_index + step_y) % NY
            projected = projected + weights_x[step_x + 1] * weights_y[step_y + 1] * jnp.take(flattened, index.astype(jnp.int32), axis=1)
    normal = jnp.dot((projected / obs_error).astype(jnp.float32), projected.T.astype(jnp.float32), precision=highest, preferred_element_type=jnp.float32) / float(NOBS)
    identity = jnp.eye(K, dtype=jnp.float32)
    lower = jnp.linalg.cholesky(gram)
    inv_lower = lax.linalg.triangular_solve(lower, identity, left_side=True, lower=True)
    system = identity + jnp.dot(jnp.dot(inv_lower, normal, precision=highest), inv_lower.T, precision=highest)
    factor = jnp.linalg.cholesky(system)
    inv_factor = lax.linalg.triangular_solve(factor, identity, left_side=True, lower=True)
    combo = jnp.dot(inv_factor, inv_lower, precision=highest)
    analysis = jnp.dot(combo.astype(jnp.float32), flattened.astype(jnp.float32), precision=highest, preferred_element_type=jnp.float32).reshape(bred.shape)
    obs_perturb = jnp.dot(combo.astype(jnp.float32), projected.astype(jnp.float32), precision=highest, preferred_element_type=jnp.float32) / jnp.sqrt(obs_error)
    return (analysis, obs_perturb)
```

```python
import functools

import jax
import jax.numpy as jnp
from jax import lax
from jax.experimental import pallas as pl
from jax.experimental.pallas import tpu as pltpu
from jax.sharding import Mesh
from jax.sharding import PartitionSpec as P

K = 8
L = 4
PLANES = 3 * L
ROWS = 8
COLS = 128
OBS = 4096
GX = ("z_lo", "y")
GY = ("z_hi", "x", "core")
GX_GY = GX + GY
FLAT = ("y", "x", "core")
DEEP = ("z_lo", "z_hi")
FIELDS = K * PLANES + PLANES
HALF = FIELDS // 2
GROUPS = 4
PER_GROUP = FIELDS // GROUPS
CHUNK = 256
BATCH = 2
STEP = 0.35
F32 = jnp.float32
highest = lax.Precision.HIGHEST


def iota(shape, dim):
    return lax.broadcasted_iota(jnp.int32, shape, dim)


def roll(x, shift, axis):
    axis = axis % x.ndim
    shift = shift % x.shape[axis]
    return x if shift == 0 else pltpu.roll(x, shift, axis)


def odd_row():
    return lax.rem(lax.axis_index("y"), 2) == 1


def odd_col():
    return lax.axis_index("core") == 1


def pack_rows_kernel(vec_ref, back_ref, one_ref, two_ref, all_ref):
    odd = odd_row()
    all_ref[0 : K * PLANES] = vec_ref[...]
    all_ref[K * PLANES : FIELDS] = back_ref[...]
    first = all_ref[0:HALF]
    second = roll(all_ref[HALF:FIELDS], 4, 1)
    top = iota((HALF, ROWS, COLS), 1) < 4
    down = jnp.where(top, first, second)
    up = jnp.where(top, second, first)
    one_ref[...] = jnp.where(odd, down, up)
    two_ref[...] = jnp.where(odd, up, down)


def pack_cols_kernel(vec_ref, back_ref, got_one, got_two, ext_ref, one_ref, two_ref):
    at_odd_row = odd_row()
    at_odd_col = odd_col()
    ext_ref[0 : K * PLANES, 0:ROWS] = vec_ref[...]
    ext_ref[K * PLANES : FIELDS, 0:ROWS] = back_ref[...]
    top = iota((HALF, ROWS, COLS), 1) < 4
    low = jnp.where(at_odd_row, got_one[...], got_two[...])
    high = jnp.where(at_odd_row, got_two[...], got_one[...])
    ext_ref[0:HALF, ROWS : 2 * ROWS] = jnp.where(top, high, low)
    ext_ref[HALF:FIELDS, ROWS : 2 * ROWS] = roll(jnp.where(top, low, high), 4, 1)
    lane = iota((2 * ROWS, COLS), 1)
    for group in range(GROUPS):
        up = jnp.zeros((2 * ROWS, COLS), F32)
        down = jnp.zeros((2 * ROWS, COLS), F32)
        for m in range(PER_GROUP):
            moved = roll(ext_ref[group * PER_GROUP + m], 4 * m, 1)
            down = jnp.where(lane // 4 == m, moved, down)
            up = jnp.where(lane // 4 == (m + 31) % 32, moved, up)
        one_ref[group] = jnp.where(at_odd_col, down, up)
        two_ref[group] = jnp.where(at_odd_col, up, down)


def tendency(state, back):
    wind_x, wind_y, vort = back
    east, north, height = state

    def along_x(f):
        return 0.5 * (roll(f, -1, f.ndim - 2) - roll(f, 1, f.ndim - 2))

    def along_y(f):
        return 0.5 * (roll(f, -1, f.ndim - 1) - roll(f, 1, f.ndim - 1))

    ex, nx, hx = along_x(east), along_x(north), along_x(height)
    ey, ny, hy = along_y(east), along_y(north), along_y(height)
    tend_east = -(wind_x * ex + wind_y * ey) - hx + vort * north
    tend_north = -(wind_x * nx + wind_y * ny) - hy - vort * east
    tend_height = -(wind_x * hx + wind_y * hy) - (ex + ny)
    return tend_east, tend_north, tend_height


def advance(start, back):
    one = [s + STEP * t for s, t in zip(start, tendency(start, back))]
    two = [
        0.75 * s + 0.25 * (o + STEP * t) for s, o, t in zip(start, one, tendency(one, back))
    ]
    return [
        s / 3.0 + 2.0 / 3.0 * (w + STEP * t) for s, w, t in zip(start, two, tendency(two, back))
    ]


def main_kernel(
    ext_ref, got_one, got_two, site_ref, off_ref, err_ref,
    bred_ref, scaled_ref, sums_ref,
    side_ref, rows_ref, edge_ref, table_ref, pair_ref,
):
    at_odd_col = odd_col()
    lane = iota((2 * ROWS, COLS), 1)
    for group in range(GROUPS):
        left = jnp.where(at_odd_col, got_one[group], got_two[group])
        right = jnp.where(at_odd_col, got_two[group], got_one[group])
        for m in range(PER_GROUP):
            moved = jnp.where(lane < 4, roll(right, -4 * m, 1), roll(left, -4 * m, 1))
            moved = jnp.where((lane < 4) | (lane >= COLS - 4), moved, 0.0)
            side_ref[group * PER_GROUP + m] = moved

    rows_ref[:, PLANES * ROWS + 2 * PLANES :, :] = jnp.zeros((K, COLS - 10 * PLANES, COLS), F32)
    edge_ref[:, PLANES * ROWS + 2 * PLANES :, :] = jnp.zeros((K, COLS - 10 * PLANES, COLS), F32)
    for level in range(L):
        base = K * PLANES + level
        back = [
            jnp.concatenate([ext_ref[base + c * L], side_ref[base + c * L]], axis=-1)[None]
            for c in range(3)
        ]

        def body(i, carry, level=level, back=back):
            start = []
            for c in range(3):
                parts = []
                for b in range(BATCH):
                    at = (i * BATCH + b) * PLANES + c * L + level
                    parts.append(jnp.concatenate([ext_ref[at], side_ref[at]], axis=-1)[None])
                start.append(jnp.concatenate(parts, axis=0))
            done = advance(start, back)
            for c in range(3):
                plane = c * L + level
                for b in range(BATCH):
                    k = i * BATCH + b
                    field = done[c][b]
                    main, side = field[:, :COLS], field[:, COLS:]
                    bred_ref[k * PLANES + plane] = main[:ROWS]
                    for ref, part in ((rows_ref, main), (edge_ref, side)):
                        ref[k, plane * ROWS : (plane + 1) * ROWS] = part[:ROWS]
                        at = PLANES * ROWS + plane
                        ref[k, at : at + 1] = part[2 * ROWS - 1 :]
                        at = PLANES * ROWS + PLANES + plane
                        ref[k, at : at + 1] = part[ROWS : ROWS + 1]
            return carry

        lax.fori_loop(0, K // BATCH, body, 0)

    for i in range(K):
        mine = bred_ref[i * PLANES : (i + 1) * PLANES]
        for j in range(i, K):
            other = mine if i == j else bred_ref[j * PLANES : (j + 1) * PLANES]
            row = jnp.sum(jnp.sum(mine * other, axis=0), axis=0, keepdims=True)
            pair_ref[i * K + j : i * K + j + 1] = row
            if i != j:
                pair_ref[j * K + i : j * K + i + 1] = row
    pair_ref[K * K :] = jnp.zeros((COLS - K * K, COLS), F32)
    contract_last = (((1,), (1,)), ((), ()))
    gram_row = lax.dot_general(
        jnp.ones((8, COLS), F32), pair_ref[...], contract_last,
        precision=highest, preferred_element_type=F32,
    )[0:1]

    def put(at, count, value):
        high = value.astype(jnp.bfloat16)
        low = (value - high.astype(F32)).astype(jnp.bfloat16)
        table_ref[at : at + count, 0:COLS] = high
        table_ref[at : at + count, COLS : 2 * COLS] = low

    ends = jnp.zeros((COLS, COLS), F32)
    lane = iota((COLS, COLS), 1)
    for k in range(K):
        put(k * COLS, COLS, rows_ref[k].T)
        edge = edge_ref[k]
        ends = jnp.where(lane == k, roll(edge, k + 1, 1), ends)
        ends = jnp.where(lane == K + k, roll(edge, K + k, 1), ends)
    put(K * COLS, 2 * K, ends.T[: 2 * K])

    def sample(step, carry):
        at = pl.multiple_of(step * CHUNK, CHUNK)
        site = site_ref[:, pl.ds(at, CHUNK)]
        shift_x = off_ref[0:1, pl.ds(at, CHUNK)]
        shift_y = off_ref[1:2, pl.ds(at, CHUNK)]
        row_at = site // COLS
        plane = site // (ROWS * COLS)
        row = row_at % ROWS
        col = site % COLS
        size_x = jnp.abs(shift_x)
        size_y = jnp.abs(shift_y)
        before = jnp.where(row == 0, PLANES * ROWS + plane, row_at - 1)
        after = jnp.where(row == ROWS - 1, PLANES * ROWS + PLANES + plane, row_at + 1)
        beside = jnp.where(shift_x < 0.0, before, after)
        next_col = jnp.where(shift_y < 0.0, col - 1, col + 1)
        own_x = 1.0 - size_x
        own_y = 1.0 - size_y

        def split(value):
            high = value.astype(jnp.bfloat16).astype(F32)
            return high, value - high

        own_high, own_low = split(own_x)
        side_high, side_low = split(size_x)
        index = iota((COLS, CHUNK), 0)
        at_own = index == row_at
        at_side = index == beside
        pick_high = jnp.where(at_own, own_high, jnp.where(at_side, side_high, 0.0))
        pick_low = jnp.where(at_own, own_low, jnp.where(at_side, side_low, 0.0))
        pick_high = pick_high.astype(jnp.bfloat16)
        pick_low = pick_low.astype(jnp.bfloat16)
        weight = jnp.where(index == col, own_y, jnp.where(index == next_col, size_y, 0.0))
        high2 = jnp.concatenate([pick_high, pick_high], axis=0)
        low2 = jnp.concatenate([pick_low, pick_low], axis=0)

        def mixed(start, count):
            part = table_ref[start : start + count]
            return jnp.dot(part, high2, preferred_element_type=F32) + jnp.dot(
                part, low2, preferred_element_type=F32
            )

        out = jnp.zeros((K, CHUNK), F32)
        sub = iota((K, CHUNK), 0)
        for k in range(K):
            line = jnp.sum(mixed(k * COLS, COLS) * weight, axis=0, keepdims=True)
            out = jnp.where(sub == k, line, out)
        ends_at = mixed(K * COLS, 2 * K)
        out = out + ends_at[:K] * jnp.where(next_col == -1, size_y, 0.0)
        out = out + ends_at[K:] * jnp.where(next_col == COLS, size_y, 0.0)
        scaled_ref[:, pl.ds(at, CHUNK)] = out / jnp.sqrt(err_ref[:, pl.ds(at, CHUNK)])
        return carry

    lax.fori_loop(0, OBS // CHUNK, sample, 0)

    scaled = scaled_ref[...]
    normal = lax.dot_general(
        scaled, scaled, contract_last, precision=highest, preferred_element_type=F32
    )
    row = gram_row
    wide = jnp.concatenate([normal, jnp.zeros((K, COLS - K), F32)], axis=1)
    for i in range(K):
        row = row + roll(wide[i : i + 1], K * K + K * i, 1)
    sums_ref[...] = row


def inverse_of_factor(a):
    n = len(a)
    low = [[None] * n for _ in range(n)]
    inv = [[None] * n for _ in range(n)]
    for j in range(n):
        total = a[j][j]
        for k in range(j):
            total = total - low[j][k] * low[j][k]
        root = jnp.sqrt(total)
        inv[j][j] = 1.0 / root
        for i in range(j + 1, n):
            total = a[i][j]
            for k in range(j):
                total = total - low[i][k] * low[j][k]
            low[i][j] = total * inv[j][j]
    for j in range(n):
        for i in range(j + 1, n):
            total = low[i][j] * inv[j][j]
            for k in range(j + 1, i):
                total = total + low[i][k] * inv[k][j]
            inv[i][j] = -total * inv[i][i]
    return inv


def added(terms):
    total = terms[0]
    for term in terms[1:]:
        total = total + term
    return total


def final_kernel(cells_all, obs_all, sums_ref, bred_ref, scaled_ref, analysis_ref, perturb_ref):
    row = sums_ref[...]
    tile = (ROWS, COLS)

    def entry(at):
        return jnp.broadcast_to(row[:, at : at + 1], tile)

    gram = [[entry(i * K + j) / cells_all if j <= i else None for j in range(K)] for i in range(K)]
    normal = [[None] * K for _ in range(K)]
    for i in range(K):
        for j in range(i + 1):
            normal[i][j] = normal[j][i] = entry(K * K + i * K + j) / obs_all
    inv_lower = inverse_of_factor(gram)
    half = [
        [added([inv_lower[i][k] * normal[k][j] for k in range(i + 1)]) for j in range(K)]
        for i in range(K)
    ]
    system = [
        [
            added([half[i][k] * inv_lower[j][k] for k in range(j + 1)]) + (1.0 if i == j else 0.0)
            for j in range(i + 1)
        ]
        for i in range(K)
    ]
    inv_factor = inverse_of_factor(system)
    combo = [
        [added([inv_factor[i][k] * inv_lower[k][j] for k in range(j, i + 1)]) for j in range(i + 1)]
        for i in range(K)
    ]
    for plane in range(PLANES):
        fields = [bred_ref[j * PLANES + plane] for j in range(K)]
        for k in range(K):
            analysis_ref[k * PLANES + plane] = added(
                [combo[k][j] * fields[j] for j in range(k + 1)]
            )
    sub = iota(tile, 0)
    columns = []
    for j in range(K):
        column = jnp.zeros(tile, F32)
        for k in range(j, K):
            column = jnp.where(sub == k, combo[k][j], column)
        columns.append(column)
    for at in range(0, OBS, COLS):
        part = scaled_ref[:, at : at + COLS]
        perturb_ref[:, at : at + COLS] = added(
            [columns[j] * part[j : j + 1] for j in range(K)]
        )


def shape(*dims):
    return jax.ShapeDtypeStruct(dims, F32)


def swap(packed, axes):
    count = lax.axis_size(axes)
    first = [(i, i ^ 1) for i in range(count)]
    second = [((i - 1) % count, ((i ^ 1) - 1) % count) for i in range(count)]
    return lax.ppermute(packed[0], axes, first), lax.ppermute(packed[1], axes, second)


def small(mib):
    return pltpu.CompilerParams(vmem_limit_bytes=mib << 20)


def spread(row, axes):
    count = lax.axis_size(axes)
    copies = jnp.broadcast_to(row[None], (count, 1, COLS))
    return lax.all_to_all(copies, axes, 0, 0, tiled=True).sum(axis=0)


def local(vectors, background, obs_site, obs_offset, obs_error):
    devices_all = lax.axis_size(GX) * lax.axis_size(GY)
    cells_all = float(PLANES * ROWS * COLS * devices_all)
    obs_all = float(OBS * devices_all)
    vec = vectors.reshape(K * PLANES, ROWS, COLS)
    back = background.reshape(PLANES, ROWS, COLS)
    packed = pl.pallas_call(
        pack_rows_kernel,
        out_shape=(shape(HALF, ROWS, COLS),) * 2,
        scratch_shapes=[pltpu.VMEM((FIELDS, ROWS, COLS), F32)],
        compiler_params=small(8),
        name="pack_rows",
    )(vec, back)
    got = swap(packed, GX)
    ext, *packed = pl.pallas_call(
        pack_cols_kernel,
        out_shape=(shape(FIELDS, 2 * ROWS, COLS),) + (shape(GROUPS, 2 * ROWS, COLS),) * 2,
        compiler_params=small(8),
        name="pack_cols",
    )(vec, back, *got)
    got = swap(packed, GY)
    bred, scaled, sums = pl.pallas_call(
        main_kernel,
        out_shape=(shape(K * PLANES, ROWS, COLS), shape(K, OBS), shape(1, COLS)),
        scratch_shapes=[
            pltpu.VMEM((FIELDS, 2 * ROWS, COLS), F32),
            pltpu.VMEM((K, COLS, COLS), F32),
            pltpu.VMEM((K, COLS, COLS), F32),
            pltpu.VMEM((K * COLS + 2 * K, 2 * COLS), jnp.bfloat16),
            pltpu.VMEM((COLS, COLS), F32),
        ],
        compiler_params=small(16),
        name="advance_sample",
    )(ext, *got, obs_site.reshape(1, OBS), obs_offset, obs_error.reshape(1, OBS))
    sums = spread(spread(sums, FLAT), DEEP)
    analysis, perturb = pl.pallas_call(
        functools.partial(final_kernel, cells_all, obs_all),
        out_shape=(shape(K * PLANES, ROWS, COLS), shape(K, OBS)),
        compiler_params=small(8),
        name="combine",
    )(sums, bred, scaled)
    return (analysis.reshape(vectors.shape), perturb)


def solution(mesh):
    torus = Mesh(mesh.devices.reshape(8, 4, 2, 4, 2), GX_GY)
    return jax.shard_map(
        local,
        mesh=torus,
        in_specs=(
            P(None, None, None, GX, GY),
            P(None, None, GX, GY),
            P(GX_GY),
            P(None, GX_GY),
            P(GX_GY),
        ),
        out_specs=(P(None, None, None, GX, GY), P(None, GX_GY)),
        check_vma=False,
    )
```

```python
import functools

import jax
import jax.numpy as jnp
from jax import lax
from jax.experimental import pallas as pl
from jax.experimental.pallas import tpu as pltpu
from jax.sharding import Mesh
from jax.sharding import PartitionSpec as P

K = 8
L = 4
PLANES = 3 * L
ROWS = 8
COLS = 128
OBS = 4096
GX = ("z_lo", "y")
GY = ("z_hi", "x", "core")
GX_GY = GX + GY
FLAT = ("y", "x", "core")
DEEP = ("z_lo", "z_hi")
FIELDS = K * PLANES + PLANES
HALF = FIELDS // 2
GROUPS = 4
STRIPS = 2 * PLANES + L
CHUNK = 512
BATCH = 4
OWN = PLANES * ROWS
STEP = 0.35
F32 = jnp.float32
highest = lax.Precision.HIGHEST


def iota(shape, dim):
    return lax.broadcasted_iota(jnp.int32, shape, dim)


def roll(x, shift, axis):
    axis = axis % x.ndim
    shift = shift % x.shape[axis]
    return x if shift == 0 else pltpu.roll(x, shift, axis)


def odd_row():
    return lax.rem(lax.axis_index("y"), 2) == 1


def odd_col():
    return lax.axis_index("core") == 1


def pack_rows_kernel(vec_ref, back_ref, one_ref, two_ref, all_ref):
    odd = odd_row()
    all_ref[0 : K * PLANES] = vec_ref[...]
    all_ref[K * PLANES : FIELDS] = back_ref[...]
    first = all_ref[0:HALF]
    second = roll(all_ref[HALF:FIELDS], 4, 1)
    top = iota((HALF, ROWS, COLS), 1) < 4
    down = jnp.where(top, first, second)
    up = jnp.where(top, second, first)
    one_ref[...] = jnp.where(odd, down, up)
    two_ref[...] = jnp.where(odd, up, down)


def pack_cols_kernel(vec_ref, back_ref, got_one, got_two, ext_ref, strip_ref, one_ref, two_ref):
    at_odd_row = odd_row()
    at_odd_col = odd_col()
    ext_ref[0 : K * PLANES, 0:ROWS] = vec_ref[...]
    ext_ref[K * PLANES : FIELDS, 0:ROWS] = back_ref[...]
    top = iota((HALF, ROWS, COLS), 1) < 4
    low = jnp.where(at_odd_row, got_one[...], got_two[...])
    high = jnp.where(at_odd_row, got_two[...], got_one[...])
    ext_ref[0:HALF, ROWS : 2 * ROWS] = jnp.where(top, high, low)
    ext_ref[HALF:FIELDS, ROWS : 2 * ROWS] = roll(jnp.where(top, low, high), 4, 1)
    lane = iota((2 * ROWS, COLS), 1)
    eighth = lax.rem(lane, 32) // 4
    for group in range(GROUPS):
        up = jnp.zeros((2 * ROWS, COLS), F32)
        down = jnp.zeros((2 * ROWS, COLS), F32)
        for u in range(8):
            t = group * 8 + u
            if t >= STRIPS:
                break
            strip = jnp.zeros((2 * ROWS, COLS), F32)
            for kk, field in enumerate(strip_fields(t)):
                plane = ext_ref[field]
                left = (lane >= 32 * kk + 4) & (lane < 32 * kk + 16)
                right = (lane >= 32 * kk + 16) & (lane < 32 * kk + 28)
                strip = jnp.where(left, roll(plane, 32 * kk + 4, 1), strip)
                strip = jnp.where(right, roll(plane, 32 * kk + 28, 1), strip)
            strip_ref[t] = strip
            down = jnp.where(eighth == u, roll(strip, 4 * u - 4, 1), down)
            up = jnp.where(eighth == u, roll(strip, 4 * u - 24, 1), up)
        one_ref[group] = jnp.where(at_odd_col, down, up)
        two_ref[group] = jnp.where(at_odd_col, up, down)


def strip_fields(t):
    if t < 2 * PLANES:
        plane, half = t // 2, t % 2
        return [(half * 4 + kk) * PLANES + plane for kk in range(4)]
    return [K * PLANES + c * L + t - 2 * PLANES for c in range(3)]


def tendency(state, back):
    wind_x, wind_y, vort = back
    east, north, height = state

    def along_x(f):
        return 0.5 * (roll(f, -1, f.ndim - 2) - roll(f, 1, f.ndim - 2))

    def along_y(f):
        return 0.5 * (roll(f, -1, f.ndim - 1) - roll(f, 1, f.ndim - 1))

    ex, nx, hx = along_x(east), along_x(north), along_x(height)
    ey, ny, hy = along_y(east), along_y(north), along_y(height)
    tend_east = -(wind_x * ex + wind_y * ey) - hx + vort * north
    tend_north = -(wind_x * nx + wind_y * ny) - hy - vort * east
    tend_height = -(wind_x * hx + wind_y * hy) - (ex + ny)
    return tend_east, tend_north, tend_height


def advance(start, back):
    one = [s + STEP * t for s, t in zip(start, tendency(start, back))]
    two = [
        0.75 * s + 0.25 * (o + STEP * t) for s, o, t in zip(start, one, tendency(one, back))
    ]
    return [
        s / 3.0 + 2.0 / 3.0 * (w + STEP * t) for s, w, t in zip(start, two, tendency(two, back))
    ]


def put_rows(ref, k, plane, field):
    ref[k, plane * ROWS : (plane + 1) * ROWS] = field[:ROWS]
    ref[k, OWN + plane : OWN + plane + 1] = field[2 * ROWS - 1 :]
    ref[k, OWN + PLANES + plane : OWN + PLANES + plane + 1] = field[ROWS : ROWS + 1]


def advance_kernel(ext_ref, rows_ref):
    rows_ref[:, OWN + 2 * PLANES :] = jnp.zeros((K, COLS - OWN - 2 * PLANES, COLS), F32)
    for level in range(L):
        base = K * PLANES + level
        back = [ext_ref[base + c * L][None] for c in range(3)]

        def body(i, carry, level=level, back=back):
            start = [
                jnp.stack(
                    [ext_ref[(i * BATCH + b) * PLANES + c * L + level] for b in range(BATCH)]
                )
                for c in range(3)
            ]
            done = advance(start, back)
            for c in range(3):
                for b in range(BATCH):
                    put_rows(rows_ref, i * BATCH + b, c * L + level, done[c][b])
            return carry

        lax.fori_loop(0, K // BATCH, body, 0)


def weights_kernel(site_ref, off_ref, err_ref, pick_ref, weight_ref, ends_ref):
    def step(i, carry):
        at = pl.ds(pl.multiple_of(i * CHUNK, CHUNK), CHUNK)
        site = site_ref[:, at]
        shift_x = off_ref[0:1, at]
        shift_y = off_ref[1:2, at]
        row_at = site // COLS
        plane = site // (ROWS * COLS)
        row = row_at % ROWS
        col = site % COLS
        size_x = jnp.abs(shift_x)
        size_y = jnp.abs(shift_y)
        before = jnp.where(row == 0, OWN + plane, row_at - 1)
        after = jnp.where(row == ROWS - 1, OWN + PLANES + plane, row_at + 1)
        beside = jnp.where(shift_x < 0.0, before, after)
        next_col = jnp.where(shift_y < 0.0, col - 1, col + 1)
        own_x = 1.0 - size_x
        scale = 1.0 / jnp.sqrt(err_ref[:, at])
        own_y = (1.0 - size_y) * scale
        side_y = size_y * scale

        def split(value):
            high = value.astype(jnp.bfloat16).astype(F32)
            return high, value - high

        own_high, own_low = split(own_x)
        side_high, side_low = split(size_x)
        index = iota((COLS, CHUNK), 0)
        at_own = index == row_at
        at_side = index == beside
        pick_high = jnp.where(at_own, own_high, jnp.where(at_side, side_high, 0.0))
        pick_low = jnp.where(at_own, own_low, jnp.where(at_side, side_low, 0.0))
        pick_ref[0:COLS, at] = pick_high.astype(jnp.bfloat16)
        pick_ref[COLS : 2 * COLS, at] = pick_low.astype(jnp.bfloat16)
        weight_ref[:, at] = jnp.where(
            index == col, own_y, jnp.where(index == next_col, side_y, 0.0)
        )
        ends_ref[0:1, at] = jnp.where(next_col == -1, side_y, 0.0)
        ends_ref[1:2, at] = jnp.where(next_col == COLS, side_y, 0.0)
        return carry

    lax.fori_loop(0, OBS // CHUNK, step, 0)


def main_kernel(
    rows_ref, strip_ref, got_one, got_two, pick_ref, weight_ref, ends_ref,
    bred_ref, scaled_ref, sums_ref,
    whole_ref, side_ref, table_ref, pair_ref,
):
    at_odd_col = odd_col()
    lane = iota((2 * ROWS, COLS), 1)
    eighth = lax.rem(lane, 32) // 4
    for group in range(GROUPS):
        left = jnp.where(at_odd_col, got_one[group], got_two[group])
        right = jnp.where(at_odd_col, got_two[group], got_one[group])
        for u in range(8):
            t = group * 8 + u
            if t >= STRIPS:
                break
            strip = jnp.where(eighth == 0, roll(left, -4 * u, 1), strip_ref[t])
            whole_ref[t] = jnp.where(eighth == 7, roll(right, 28 - 4 * u, 1), strip)
    side_ref[:, OWN + 2 * PLANES :] = jnp.zeros((2, COLS - OWN - 2 * PLANES, COLS), F32)
    for level in range(L):
        mixed_back = whole_ref[2 * PLANES + level]
        back = []
        for c in range(3):
            spread_back = mixed_back
            for kk in range(4):
                if kk != c:
                    spread_back = jnp.where(
                        lane // 32 == kk, roll(mixed_back, 32 * (kk - c), 1), spread_back
                    )
            back.append(spread_back[None])
        start = [
            whole_ref[2 * (c * L + level) : 2 * (c * L + level) + 2] for c in range(3)
        ]
        done = advance(start, back)
        for c in range(3):
            for half in range(2):
                put_rows(side_ref, half, c * L + level, done[c][half])

    def put(at, count, value):
        high = value.astype(jnp.bfloat16)
        low = (value - high.astype(F32)).astype(jnp.bfloat16)
        table_ref[at : at + count, 0:COLS] = high
        table_ref[at : at + count, COLS : 2 * COLS] = low

    lane = iota((COLS, COLS), 1)
    for k in range(K):
        side, kk = side_ref[k // 4], k % 4
        fields = jnp.where(lane < 3, roll(side, -(32 * kk + 4), 1), rows_ref[k])
        fields = jnp.where(lane >= COLS - 3, roll(side, 100 - 32 * kk, 1), fields)
        bred_ref[k * PLANES : (k + 1) * PLANES] = fields[:OWN].reshape(PLANES, ROWS, COLS)
        put(k * COLS, COLS, fields.T)
    across = [side_ref[half].T for half in range(2)]
    lines = [across[k // 4][32 * (k % 4) + 3 :][:1] for k in range(K)]
    lines += [across[k // 4][32 * (k % 4) + 28 :][:1] for k in range(K)]
    put(K * COLS, 2 * K, jnp.concatenate(lines, axis=0))

    for i in range(K):
        mine = bred_ref[i * PLANES : (i + 1) * PLANES]
        for j in range(i, K):
            other = mine if i == j else bred_ref[j * PLANES : (j + 1) * PLANES]
            row = jnp.sum(jnp.sum(mine * other, axis=0), axis=0, keepdims=True)
            pair_ref[i * K + j : i * K + j + 1] = row
            if i != j:
                pair_ref[j * K + i : j * K + i + 1] = row
    pair_ref[K * K :] = jnp.zeros((COLS - K * K, COLS), F32)
    contract_last = (((1,), (1,)), ((), ()))
    gram_row = lax.dot_general(
        jnp.ones((8, COLS), F32), pair_ref[...], contract_last,
        precision=highest, preferred_element_type=F32,
    )[0:1]

    def sample(step, carry):
        at = pl.ds(pl.multiple_of(step * CHUNK, CHUNK), CHUNK)
        high, low = pick_ref[0:COLS, at], pick_ref[COLS : 2 * COLS, at]
        high2 = jnp.concatenate([high, high], axis=0)
        low2 = jnp.concatenate([low, low], axis=0)
        weight = weight_ref[:, at]

        def mixed(start, count):
            part = table_ref[start : start + count]
            return jnp.dot(part, high2, preferred_element_type=F32) + jnp.dot(
                part, low2, preferred_element_type=F32
            )

        out = jnp.zeros((K, CHUNK), F32)
        sub = iota((K, CHUNK), 0)
        for k in range(K):
            line = jnp.sum(mixed(k * COLS, COLS) * weight, axis=0, keepdims=True)
            out = jnp.where(sub == k, line, out)
        ends_at = mixed(K * COLS, 2 * K)
        out = out + ends_at[:K] * ends_ref[0:1, at]
        out = out + ends_at[K:] * ends_ref[1:2, at]
        scaled_ref[:, at] = out
        return carry

    lax.fori_loop(0, OBS // CHUNK, sample, 0)

    scaled = scaled_ref[...]
    normal = lax.dot_general(
        scaled, scaled, contract_last, precision=highest, preferred_element_type=F32
    )
    row = gram_row
    wide = jnp.concatenate([normal, jnp.zeros((K, COLS - K), F32)], axis=1)
    for i in range(K):
        row = row + roll(wide[i : i + 1], K * K + K * i, 1)
    sums_ref[...] = row


def inverse_of_factor(a):
    n = len(a)
    low = [[None] * n for _ in range(n)]
    inv = [[None] * n for _ in range(n)]
    for j in range(n):
        total = a[j][j]
        for k in range(j):
            total = total - low[j][k] * low[j][k]
        root = jnp.sqrt(total)
        inv[j][j] = 1.0 / root
        for i in range(j + 1, n):
            total = a[i][j]
            for k in range(j):
                total = total - low[i][k] * low[j][k]
            low[i][j] = total * inv[j][j]
    for j in range(n):
        for i in range(j + 1, n):
            total = low[i][j] * inv[j][j]
            for k in range(j + 1, i):
                total = total + low[i][k] * inv[k][j]
            inv[i][j] = -total * inv[i][i]
    return inv


def added(terms):
    total = terms[0]
    for term in terms[1:]:
        total = total + term
    return total


def final_kernel(cells_all, obs_all, sums_ref, bred_ref, scaled_ref, analysis_ref, perturb_ref):
    row = sums_ref[...]
    tile = (ROWS, COLS)

    def entry(at):
        return jnp.broadcast_to(row[:, at : at + 1], tile)

    gram = [[entry(i * K + j) / cells_all if j <= i else None for j in range(K)] for i in range(K)]
    normal = [[None] * K for _ in range(K)]
    for i in range(K):
        for j in range(i + 1):
            normal[i][j] = normal[j][i] = entry(K * K + i * K + j) / obs_all
    inv_lower = inverse_of_factor(gram)
    half = [
        [added([inv_lower[i][k] * normal[k][j] for k in range(i + 1)]) for j in range(K)]
        for i in range(K)
    ]
    system = [
        [
            added([half[i][k] * inv_lower[j][k] for k in range(j + 1)]) + (1.0 if i == j else 0.0)
            for j in range(i + 1)
        ]
        for i in range(K)
    ]
    inv_factor = inverse_of_factor(system)
    combo = [
        [added([inv_factor[i][k] * inv_lower[k][j] for k in range(j, i + 1)]) for j in range(i + 1)]
        for i in range(K)
    ]
    for plane in range(PLANES):
        fields = [bred_ref[j * PLANES + plane] for j in range(K)]
        for k in range(K):
            analysis_ref[k * PLANES + plane] = added(
                [combo[k][j] * fields[j] for j in range(k + 1)]
            )
    sub = iota(tile, 0)
    columns = []
    for j in range(K):
        column = jnp.zeros(tile, F32)
        for k in range(j, K):
            column = jnp.where(sub == k, combo[k][j], column)
        columns.append(column)
    for at in range(0, OBS, COLS):
        part = scaled_ref[:, at : at + COLS]
        perturb_ref[:, at : at + COLS] = added(
            [columns[j] * part[j : j + 1] for j in range(K)]
        )


def shape(*dims):
    return jax.ShapeDtypeStruct(dims, F32)


def swap(packed, axes):
    count = lax.axis_size(axes)
    first = [(i, i ^ 1) for i in range(count)]
    second = [((i - 1) % count, ((i ^ 1) - 1) % count) for i in range(count)]
    other = lax.ppermute(packed[1], axes, second)
    return lax.ppermute(packed[0], axes, first), other


def small(mib):
    return pltpu.CompilerParams(vmem_limit_bytes=mib << 20)


def spread(row, axes):
    count = lax.axis_size(axes)
    copies = jnp.broadcast_to(row[None], (count, 1, COLS))
    return lax.all_to_all(copies, axes, 0, 0, tiled=True).sum(axis=0)


def main_call(*operands):
    return pl.pallas_call(
        main_kernel,
        out_shape=(shape(K * PLANES, ROWS, COLS), shape(K, OBS), shape(1, COLS)),
        scratch_shapes=[
            pltpu.VMEM((STRIPS, 2 * ROWS, COLS), F32),
            pltpu.VMEM((2, COLS, COLS), F32),
            pltpu.VMEM((K * COLS + 2 * K, 2 * COLS), jnp.bfloat16),
            pltpu.VMEM((COLS, COLS), F32),
        ],
        compiler_params=small(16),
        name="advance_sample",
    )(*operands)


def busy(us):
    return pl.CostEstimate(flops=us * 10**9, bytes_accessed=0, transcendentals=0)


def local(vectors, background, obs_site, obs_offset, obs_error):
    devices_all = lax.axis_size(GX) * lax.axis_size(GY)
    cells_all = float(PLANES * ROWS * COLS * devices_all)
    obs_all = float(OBS * devices_all)
    vec = vectors.reshape(K * PLANES, ROWS, COLS)
    back = background.reshape(PLANES, ROWS, COLS)
    packed = pl.pallas_call(
        pack_rows_kernel,
        out_shape=(shape(HALF, ROWS, COLS),) * 2,
        scratch_shapes=[pltpu.VMEM((FIELDS, ROWS, COLS), F32)],
        compiler_params=small(8),
        name="pack_rows",
    )(vec, back)
    got = swap(packed, GX)
    weights = pl.pallas_call(
        weights_kernel,
        out_shape=(
            jax.ShapeDtypeStruct((2 * COLS, OBS), jnp.bfloat16), shape(COLS, OBS), shape(2, OBS)
        ),
        compiler_params=small(8),
        cost_estimate=busy(3),
        name="weights",
    )(obs_site.reshape(1, OBS), obs_offset, obs_error.reshape(1, OBS))
    ext, strips, *packed = pl.pallas_call(
        pack_cols_kernel,
        out_shape=(shape(FIELDS, 2 * ROWS, COLS), shape(STRIPS, 2 * ROWS, COLS))
        + (shape(GROUPS, 2 * ROWS, COLS),) * 2,
        compiler_params=small(8),
        name="pack_cols",
    )(vec, back, *got)
    got = swap(packed, GY)
    rows = pl.pallas_call(
        advance_kernel,
        out_shape=shape(K, COLS, COLS),
        compiler_params=small(8),
        cost_estimate=busy(3),
        name="advance",
    )(ext)
    bred, scaled, sums = main_call(rows, strips, *got, *weights)
    sums = spread(spread(sums, FLAT), DEEP)
    analysis, perturb = pl.pallas_call(
        functools.partial(final_kernel, cells_all, obs_all),
        out_shape=(shape(K * PLANES, ROWS, COLS), shape(K, OBS)),
        compiler_params=small(8),
        name="combine",
    )(sums, bred, scaled)
    return (analysis.reshape(vectors.shape), perturb)


def solution(mesh):
    torus = Mesh(mesh.devices.reshape(8, 4, 2, 4, 2), GX_GY)
    return jax.shard_map(
        local,
        mesh=torus,
        in_specs=(
            P(None, None, None, GX, GY),
            P(None, None, GX, GY),
            P(GX_GY),
            P(None, GX_GY),
            P(GX_GY),
        ),
        out_specs=(P(None, None, None, GX, GY), P(None, GX_GY)),
        check_vma=False,
    )
```

```python
import functools

import jax
import jax.numpy as jnp
from jax import lax
from jax.experimental import pallas as pl
from jax.experimental.pallas import tpu as pltpu
from jax.sharding import Mesh
from jax.sharding import PartitionSpec as P

K = 8
L = 4
PLANES = 3 * L
ROWS = 8
COLS = 128
OBS = 4096
GX = ("z_lo", "y")
GY = ("z_hi", "x", "core")
GX_GY = GX + GY
FLAT = ("y", "x", "core")
DEEP = ("z_lo", "z_hi")
FIELDS = K * PLANES + PLANES
HALF = FIELDS // 2
GROUPS = 4
STRIPS = 2 * PLANES + L
CHUNK = 512
BATCH = 4
OWN = PLANES * ROWS
STEP = 0.35
F32 = jnp.float32
highest = lax.Precision.HIGHEST


def iota(shape, dim):
    return lax.broadcasted_iota(jnp.int32, shape, dim)


def roll(x, shift, axis):
    axis = axis % x.ndim
    shift = shift % x.shape[axis]
    return x if shift == 0 else pltpu.roll(x, shift, axis)


def odd_row():
    return lax.rem(lax.axis_index("y"), 2) == 1


def odd_col():
    return lax.axis_index("core") == 1


def pack_rows_kernel(vec_ref, back_ref, all_ref, one_ref, two_ref):
    odd = odd_row()
    all_ref[0 : K * PLANES] = vec_ref[...]
    all_ref[K * PLANES : FIELDS] = back_ref[...]
    first = all_ref[0:HALF]
    second = roll(all_ref[HALF:FIELDS], 4, 1)
    top = iota((HALF, ROWS, COLS), 1) < 4
    down = jnp.where(top, first, second)
    up = jnp.where(top, second, first)
    one_ref[...] = jnp.where(odd, down, up)
    two_ref[...] = jnp.where(odd, up, down)


def pack_cols_kernel(own_ref, got_one, got_two, ext_ref, strip_ref, one_ref, two_ref):
    at_odd_row = odd_row()
    at_odd_col = odd_col()
    ext_ref[:, 0:ROWS] = own_ref[...]
    top = iota((HALF, ROWS, COLS), 1) < 4
    low = jnp.where(at_odd_row, got_one[...], got_two[...])
    high = jnp.where(at_odd_row, got_two[...], got_one[...])
    ext_ref[0:HALF, ROWS : 2 * ROWS] = jnp.where(top, high, low)
    ext_ref[HALF:FIELDS, ROWS : 2 * ROWS] = roll(jnp.where(top, low, high), 4, 1)
    lane = iota((2 * ROWS, COLS), 1)
    eighth = lax.rem(lane, 32) // 4
    for group in range(GROUPS):
        up = jnp.zeros((2 * ROWS, COLS), F32)
        down = jnp.zeros((2 * ROWS, COLS), F32)
        first, last = group * 8, min(group * 8 + 8, STRIPS)
        planes = {f: ext_ref[f] for t in range(first, last) for f in strip_fields(t)}
        strips = []
        for t in range(first, last):
            u = t - first
            strip = jnp.zeros((2 * ROWS, COLS), F32)
            for kk, field in enumerate(strip_fields(t)):
                plane = planes[field]
                left = (lane >= 32 * kk + 4) & (lane < 32 * kk + 16)
                right = (lane >= 32 * kk + 16) & (lane < 32 * kk + 28)
                strip = jnp.where(left, roll(plane, 32 * kk + 4, 1), strip)
                strip = jnp.where(right, roll(plane, 32 * kk + 28, 1), strip)
            strips.append(strip)
            down = jnp.where(eighth == u, roll(strip, 4 * u - 4, 1), down)
            up = jnp.where(eighth == u, roll(strip, 4 * u - 24, 1), up)
        for t, strip in zip(range(first, last), strips):
            strip_ref[t] = strip
        one_ref[group] = jnp.where(at_odd_col, down, up)
        two_ref[group] = jnp.where(at_odd_col, up, down)


def strip_fields(t):
    if t < 2 * PLANES:
        plane, half = t // 2, t % 2
        return [(half * 4 + kk) * PLANES + plane for kk in range(4)]
    return [K * PLANES + c * L + t - 2 * PLANES for c in range(3)]


def tendency(state, back):
    wind_x, wind_y, vort = back
    east, north, height = state

    def along_x(f):
        return 0.5 * (roll(f, -1, f.ndim - 2) - roll(f, 1, f.ndim - 2))

    def along_y(f):
        return 0.5 * (roll(f, -1, f.ndim - 1) - roll(f, 1, f.ndim - 1))

    ex, nx, hx = along_x(east), along_x(north), along_x(height)
    ey, ny, hy = along_y(east), along_y(north), along_y(height)
    tend_east = -(wind_x * ex + wind_y * ey) - hx + vort * north
    tend_north = -(wind_x * nx + wind_y * ny) - hy - vort * east
    tend_height = -(wind_x * hx + wind_y * hy) - (ex + ny)
    return tend_east, tend_north, tend_height


def advance(start, back):
    one = [s + STEP * t for s, t in zip(start, tendency(start, back))]
    two = [
        0.75 * s + 0.25 * (o + STEP * t) for s, o, t in zip(start, one, tendency(one, back))
    ]
    return [
        s / 3.0 + 2.0 / 3.0 * (w + STEP * t) for s, w, t in zip(start, two, tendency(two, back))
    ]


def put_rows(ref, k, plane, field):
    ref[k, plane * ROWS : (plane + 1) * ROWS] = field[:ROWS]
    ref[k, OWN + plane : OWN + plane + 1] = field[2 * ROWS - 1 :]
    ref[k, OWN + PLANES + plane : OWN + PLANES + plane + 1] = field[ROWS : ROWS + 1]


def advance_kernel(ext_ref, rows_ref, table_ref):
    rows_ref[:, OWN + 2 * PLANES :] = jnp.zeros((K, COLS - OWN - 2 * PLANES, COLS), F32)
    for level in range(L):
        base = K * PLANES + level
        back = [ext_ref[base + c * L][None] for c in range(3)]

        def body(i, carry, level=level, back=back):
            start = [
                jnp.stack(
                    [ext_ref[(i * BATCH + b) * PLANES + c * L + level] for b in range(BATCH)]
                )
                for c in range(3)
            ]
            done = advance(start, back)
            for c in range(3):
                for b in range(BATCH):
                    put_rows(rows_ref, i * BATCH + b, c * L + level, done[c][b])
            return carry

        lax.fori_loop(0, K // BATCH, body, 0)
    inner = iota((COLS, COLS), 1)
    inner = (inner >= 3) & (inner < COLS - 3)
    for k in range(K):
        put_table(table_ref, k * COLS, jnp.where(inner, rows_ref[k], 0.0).T)


def put_table(ref, at, value):
    high = value.astype(jnp.bfloat16)
    low = (value - high.astype(F32)).astype(jnp.bfloat16)
    ref[at : at + value.shape[0], 0:COLS] = high
    ref[at : at + value.shape[0], COLS : 2 * COLS] = low


def weights_kernel(site_ref, off_ref, err_ref, pick_ref, weight_ref, ends_ref):
    def step(i, carry):
        at = pl.ds(pl.multiple_of(i * CHUNK, CHUNK), CHUNK)
        site = site_ref[:, at]
        shift_x = off_ref[0:1, at]
        shift_y = off_ref[1:2, at]
        row_at = site // COLS
        plane = site // (ROWS * COLS)
        row = row_at % ROWS
        col = site % COLS
        size_x = jnp.abs(shift_x)
        size_y = jnp.abs(shift_y)
        before = jnp.where(row == 0, OWN + plane, row_at - 1)
        after = jnp.where(row == ROWS - 1, OWN + PLANES + plane, row_at + 1)
        beside = jnp.where(shift_x < 0.0, before, after)
        next_col = jnp.where(shift_y < 0.0, col - 1, col + 1)
        own_x = 1.0 - size_x
        scale = 1.0 / jnp.sqrt(err_ref[:, at])
        own_y = (1.0 - size_y) * scale
        side_y = size_y * scale

        def split(value):
            high = value.astype(jnp.bfloat16).astype(F32)
            return high, value - high

        own_high, own_low = split(own_x)
        side_high, side_low = split(size_x)
        index = iota((COLS, CHUNK), 0)
        at_own = index == row_at
        at_side = index == beside
        pick_high = jnp.where(at_own, own_high, jnp.where(at_side, side_high, 0.0))
        pick_low = jnp.where(at_own, own_low, jnp.where(at_side, side_low, 0.0))
        pick_ref[0:COLS, at] = pick_high.astype(jnp.bfloat16)
        pick_ref[COLS : 2 * COLS, at] = pick_low.astype(jnp.bfloat16)
        weight_ref[:, at] = jnp.where(
            index == col, own_y, jnp.where(index == next_col, side_y, 0.0)
        )
        line = iota((ROWS, CHUNK), 0)
        line = jnp.where(line < 4, line - 1, line + COLS - 7)
        ends_ref[:, at] = jnp.where(line == col, own_y, jnp.where(line == next_col, side_y, 0.0))
        return carry

    lax.fori_loop(0, OBS // CHUNK, step, 0)


def main_kernel(
    rows_ref, table_ref, strip_ref, got_one, got_two, pick_ref, weight_ref, ends_ref,
    bred_ref, scaled_ref, sums_ref,
    whole_ref, side_ref, edge_ref, pair_ref,
):
    at_odd_col = odd_col()
    lane = iota((2 * ROWS, COLS), 1)
    eighth = lax.rem(lane, 32) // 4
    for group in range(GROUPS):
        left = jnp.where(at_odd_col, got_one[group], got_two[group])
        right = jnp.where(at_odd_col, got_two[group], got_one[group])
        for u in range(8):
            t = group * 8 + u
            if t >= STRIPS:
                break
            strip = jnp.where(eighth == 0, roll(left, -4 * u, 1), strip_ref[t])
            whole_ref[t] = jnp.where(eighth == 7, roll(right, 28 - 4 * u, 1), strip)
    side_ref[:, OWN + 2 * PLANES :] = jnp.zeros((2, COLS - OWN - 2 * PLANES, COLS), F32)
    results = []
    for level in range(L):
        mixed_back = whole_ref[2 * PLANES + level]
        back = []
        for c in range(3):
            spread_back = mixed_back
            for kk in range(4):
                if kk != c:
                    spread_back = jnp.where(
                        lane // 32 == kk, roll(mixed_back, 32 * (kk - c), 1), spread_back
                    )
            back.append(spread_back[None])
        start = [
            whole_ref[2 * (c * L + level) : 2 * (c * L + level) + 2] for c in range(3)
        ]
        results.append(advance(start, back))
    for level in range(L):
        for c in range(3):
            for half in range(2):
                put_rows(side_ref, half, c * L + level, results[level][c][half])

    across = [side_ref[half].T for half in range(2)]
    lines = []
    for k in range(K):
        turned, at = across[k // 4], 32 * (k % 4)
        lines += [turned[at + 3 : at + 7], turned[at + 25 : at + 29]]
    put_table(edge_ref, 0, jnp.concatenate(lines, axis=0))
    lane = iota((OWN, COLS), 1)
    for pair in range(0, K, 2):
        fields = []
        for k in (pair, pair + 1):
            side, kk = side_ref[k // 4, 0:OWN], k % 4
            field = jnp.where(lane < 3, roll(side, -(32 * kk + 4), 1), rows_ref[k, 0:OWN])
            fields.append(jnp.where(lane >= COLS - 3, roll(side, 100 - 32 * kk, 1), field))
        for k, field in zip((pair, pair + 1), fields):
            bred_ref[k * PLANES : (k + 1) * PLANES] = field.reshape(PLANES, ROWS, COLS)

    for i in range(K):
        mine = bred_ref[i * PLANES : (i + 1) * PLANES]
        for j in range(i, K):
            other = mine if i == j else bred_ref[j * PLANES : (j + 1) * PLANES]
            row = jnp.sum(jnp.sum(mine * other, axis=0), axis=0, keepdims=True)
            pair_ref[i * K + j : i * K + j + 1] = row
            if i != j:
                pair_ref[j * K + i : j * K + i + 1] = row
    pair_ref[K * K :] = jnp.zeros((COLS - K * K, COLS), F32)
    contract_last = (((1,), (1,)), ((), ()))
    gram_row = lax.dot_general(
        jnp.ones((8, COLS), F32), pair_ref[...], contract_last,
        precision=highest, preferred_element_type=F32,
    )[0:1]

    def sample(step, carry):
        at = pl.ds(pl.multiple_of(step * CHUNK, CHUNK), CHUNK)
        high, low = pick_ref[0:COLS, at], pick_ref[COLS : 2 * COLS, at]
        high2 = jnp.concatenate([high, high], axis=0)
        low2 = jnp.concatenate([low, low], axis=0)
        weight = weight_ref[:, at]

        def mixed(part):
            return jnp.dot(part, high2, preferred_element_type=F32) + jnp.dot(
                part, low2, preferred_element_type=F32
            )

        out = jnp.zeros((K, CHUNK), F32)
        sub = iota((K, CHUNK), 0)
        ends = mixed(edge_ref[...])
        for k in range(K):
            part = mixed(table_ref[k * COLS : (k + 1) * COLS]) * weight
            part = part.reshape(COLS // ROWS, ROWS, CHUNK).sum(axis=0)
            part = part + ends[k * ROWS : (k + 1) * ROWS] * ends_ref[:, at]
            out = jnp.where(sub == k, jnp.sum(part, axis=0, keepdims=True), out)
        scaled_ref[:, at] = out
        return carry

    lax.fori_loop(0, OBS // CHUNK, sample, 0)

    scaled = scaled_ref[...]
    normal = lax.dot_general(
        scaled, scaled, contract_last, precision=highest, preferred_element_type=F32
    )
    row = gram_row
    wide = jnp.concatenate([normal, jnp.zeros((K, COLS - K), F32)], axis=1)
    for i in range(K):
        row = row + roll(wide[i : i + 1], K * K + K * i, 1)
    sums_ref[...] = row


def inverse_of_factor(a):
    n = len(a)
    low = [[None] * n for _ in range(n)]
    inv = [[None] * n for _ in range(n)]
    for j in range(n):
        total = a[j][j]
        for k in range(j):
            total = total - low[j][k] * low[j][k]
        root = jnp.sqrt(total)
        inv[j][j] = 1.0 / root
        for i in range(j + 1, n):
            total = a[i][j]
            for k in range(j):
                total = total - low[i][k] * low[j][k]
            low[i][j] = total * inv[j][j]
    for j in range(n):
        for i in range(j + 1, n):
            total = low[i][j] * inv[j][j]
            for k in range(j + 1, i):
                total = total + low[i][k] * inv[k][j]
            inv[i][j] = -total * inv[i][i]
    return inv


def added(terms):
    total = terms[0]
    for term in terms[1:]:
        total = total + term
    return total


def final_kernel(cells_all, obs_all, sums_ref, bred_ref, scaled_ref, analysis_ref, perturb_ref):
    row = sums_ref[...]
    tile = (ROWS, COLS)

    def entry(at):
        return jnp.broadcast_to(row[:, at : at + 1], tile)

    gram = [[entry(i * K + j) / cells_all if j <= i else None for j in range(K)] for i in range(K)]
    normal = [[None] * K for _ in range(K)]
    for i in range(K):
        for j in range(i + 1):
            normal[i][j] = normal[j][i] = entry(K * K + i * K + j) / obs_all
    inv_lower = inverse_of_factor(gram)
    half = [
        [added([inv_lower[i][k] * normal[k][j] for k in range(i + 1)]) for j in range(K)]
        for i in range(K)
    ]
    system = [
        [
            added([half[i][k] * inv_lower[j][k] for k in range(j + 1)]) + (1.0 if i == j else 0.0)
            for j in range(i + 1)
        ]
        for i in range(K)
    ]
    inv_factor = inverse_of_factor(system)
    combo = [
        [added([inv_factor[i][k] * inv_lower[k][j] for k in range(j, i + 1)]) for j in range(i + 1)]
        for i in range(K)
    ]
    for plane in range(PLANES):
        fields = [bred_ref[j * PLANES + plane] for j in range(K)]
        for k in range(K):
            analysis_ref[k * PLANES + plane] = added(
                [combo[k][j] * fields[j] for j in range(k + 1)]
            )
    sub = iota(tile, 0)
    columns = []
    for j in range(K):
        column = jnp.zeros(tile, F32)
        for k in range(j, K):
            column = jnp.where(sub == k, combo[k][j], column)
        columns.append(column)
    for at in range(0, OBS, COLS):
        part = scaled_ref[:, at : at + COLS]
        perturb_ref[:, at : at + COLS] = added(
            [columns[j] * part[j : j + 1] for j in range(K)]
        )


def shape(*dims):
    return jax.ShapeDtypeStruct(dims, F32)


def swap(packed, axes):
    count = lax.axis_size(axes)
    first = [(i, i ^ 1) for i in range(count)]
    second = [((i - 1) % count, ((i ^ 1) - 1) % count) for i in range(count)]
    far = lax.ppermute(packed[1], axes, second)
    near = lax.ppermute(packed[0], axes, first)
    return near, far


def small(mib):
    return pltpu.CompilerParams(vmem_limit_bytes=mib << 20)


def spread(row, axes):
    count = lax.axis_size(axes)
    copies = jnp.broadcast_to(row[None], (count, 1, COLS))
    return lax.all_to_all(copies, axes, 0, 0, tiled=True).sum(axis=0)


def main_call(*operands):
    return pl.pallas_call(
        main_kernel,
        out_shape=(shape(K * PLANES, ROWS, COLS), shape(K, OBS), shape(1, COLS)),
        scratch_shapes=[
            pltpu.VMEM((STRIPS, 2 * ROWS, COLS), F32),
            pltpu.VMEM((2, COLS, COLS), F32),
            pltpu.VMEM((K * ROWS, 2 * COLS), jnp.bfloat16),
            pltpu.VMEM((COLS, COLS), F32),
        ],
        compiler_params=small(16),
        name="advance_sample",
    )(*operands)


def busy(us):
    return pl.CostEstimate(flops=us * 10**9, bytes_accessed=0, transcendentals=0)


def local(vectors, background, obs_site, obs_offset, obs_error):
    devices_all = lax.axis_size(GX) * lax.axis_size(GY)
    cells_all = float(PLANES * ROWS * COLS * devices_all)
    obs_all = float(OBS * devices_all)
    vec = vectors.reshape(K * PLANES, ROWS, COLS)
    back = background.reshape(PLANES, ROWS, COLS)
    own, *packed = pl.pallas_call(
        pack_rows_kernel,
        out_shape=(shape(FIELDS, ROWS, COLS),) + (shape(HALF, ROWS, COLS),) * 2,
        compiler_params=small(8),
        name="pack_rows",
    )(vec, back)
    got = swap(packed, GX)
    weights = pl.pallas_call(
        weights_kernel,
        out_shape=(
            jax.ShapeDtypeStruct((2 * COLS, OBS), jnp.bfloat16), shape(COLS, OBS), shape(ROWS, OBS)
        ),
        compiler_params=small(8),
        cost_estimate=busy(3),
        name="weights",
    )(obs_site.reshape(1, OBS), obs_offset, obs_error.reshape(1, OBS))
    ext, strips, *packed = pl.pallas_call(
        pack_cols_kernel,
        out_shape=(shape(FIELDS, 2 * ROWS, COLS), shape(STRIPS, 2 * ROWS, COLS))
        + (shape(GROUPS, 2 * ROWS, COLS),) * 2,
        compiler_params=small(8),
        name="pack_cols",
    )(own, *got)
    got = swap(packed, GY)
    mine = pl.pallas_call(
        advance_kernel,
        out_shape=(
            shape(K, COLS, COLS), jax.ShapeDtypeStruct((K * COLS, 2 * COLS), jnp.bfloat16)
        ),
        compiler_params=small(8),
        cost_estimate=busy(3),
        name="advance",
    )(ext)
    bred, scaled, sums = main_call(*mine, strips, *got, *weights)
    sums = spread(spread(sums, FLAT), DEEP)
    analysis, perturb = pl.pallas_call(
        functools.partial(final_kernel, cells_all, obs_all),
        out_shape=(shape(K * PLANES, ROWS, COLS), shape(K, OBS)),
        compiler_params=small(8),
        name="combine",
    )(sums, bred, scaled)
    return (analysis.reshape(vectors.shape), perturb)


def solution(mesh):
    torus = Mesh(mesh.devices.reshape(8, 4, 2, 4, 2), GX_GY)
    return jax.shard_map(
        local,
        mesh=torus,
        in_specs=(
            P(None, None, None, GX, GY),
            P(None, None, GX, GY),
            P(GX_GY),
            P(None, GX_GY),
            P(GX_GY),
        ),
        out_specs=(P(None, None, None, GX, GY), P(None, GX_GY)),
        check_vma=False,
    )
```

```python
import functools

import jax
import jax.numpy as jnp
from jax import lax
from jax.experimental import pallas as pl
from jax.experimental.pallas import tpu as pltpu
from jax.sharding import Mesh
from jax.sharding import PartitionSpec as P

K = 8
L = 4
PLANES = 3 * L
ROWS = 8
COLS = 128
OBS = 4096
GX = ("z_lo", "y")
GY = ("z_hi", "x", "core")
GX_GY = GX + GY
FLAT = ("y", "x", "core")
DEEP = ("z_lo", "z_hi")
FIELDS = K * PLANES + PLANES
HALF = FIELDS // 2
GROUPS = 4
STRIPS = 2 * PLANES + L
CHUNK = 512
BATCH = 4
OWN = PLANES * ROWS
STEP = 0.35
F32 = jnp.float32
highest = lax.Precision.HIGHEST


def iota(shape, dim):
    return lax.broadcasted_iota(jnp.int32, shape, dim)


def roll(x, shift, axis):
    axis = axis % x.ndim
    shift = shift % x.shape[axis]
    return x if shift == 0 else pltpu.roll(x, shift, axis)


def odd_row():
    return lax.rem(lax.axis_index("y"), 2) == 1


def odd_col():
    return lax.axis_index("core") == 1


def pack_rows_kernel(vec_ref, back_ref, all_ref, one_ref, two_ref):
    odd = odd_row()
    all_ref[0 : K * PLANES] = vec_ref[...]
    all_ref[K * PLANES : FIELDS] = back_ref[...]
    first = all_ref[0:HALF]
    second = roll(all_ref[HALF:FIELDS], 4, 1)
    top = iota((HALF, ROWS, COLS), 1) < 4
    down = jnp.where(top, first, second)
    up = jnp.where(top, second, first)
    one_ref[...] = jnp.where(odd, down, up)
    two_ref[...] = jnp.where(odd, up, down)


def pack_cols_kernel(own_ref, got_one, got_two, ext_ref, one_ref, two_ref):
    at_odd_row = odd_row()
    at_odd_col = odd_col()
    ext_ref[:, 0:ROWS] = own_ref[...]
    top = iota((HALF, ROWS, COLS), 1) < 4
    low = jnp.where(at_odd_row, got_one[...], got_two[...])
    high = jnp.where(at_odd_row, got_two[...], got_one[...])
    ext_ref[0:HALF, ROWS : 2 * ROWS] = jnp.where(top, high, low)
    ext_ref[HALF:FIELDS, ROWS : 2 * ROWS] = roll(jnp.where(top, low, high), 4, 1)
    lane = iota((2 * ROWS, COLS), 1)
    for group in range(GROUPS):
        up = jnp.zeros((2 * ROWS, COLS), F32)
        down = jnp.zeros((2 * ROWS, COLS), F32)
        for u in range(min(8, STRIPS - group * 8)):
            for kk, field in enumerate(strip_fields(group * 8 + u)):
                moved = roll(ext_ref[field], 32 * kk + 4 * u, 1)
                down = jnp.where(lane // 4 == 8 * kk + u, moved, down)
                up = jnp.where(lane // 4 == (8 * kk + u + 31) % 32, moved, up)
        one_ref[group] = jnp.where(at_odd_col, down, up)
        two_ref[group] = jnp.where(at_odd_col, up, down)


def strip_fields(t):
    if t < 2 * PLANES:
        plane, half = t // 2, t % 2
        return [(half * 4 + kk) * PLANES + plane for kk in range(4)]
    return [K * PLANES + c * L + t - 2 * PLANES for c in range(3)]


def tendency(state, back):
    wind_x, wind_y, vort = back
    east, north, height = state

    def along_x(f):
        return 0.5 * (roll(f, -1, f.ndim - 2) - roll(f, 1, f.ndim - 2))

    def along_y(f):
        return 0.5 * (roll(f, -1, f.ndim - 1) - roll(f, 1, f.ndim - 1))

    ex, nx, hx = along_x(east), along_x(north), along_x(height)
    ey, ny, hy = along_y(east), along_y(north), along_y(height)
    tend_east = -(wind_x * ex + wind_y * ey) - hx + vort * north
    tend_north = -(wind_x * nx + wind_y * ny) - hy - vort * east
    tend_height = -(wind_x * hx + wind_y * hy) - (ex + ny)
    return tend_east, tend_north, tend_height


def advance(start, back):
    one = [s + STEP * t for s, t in zip(start, tendency(start, back))]
    two = [
        0.75 * s + 0.25 * (o + STEP * t) for s, o, t in zip(start, one, tendency(one, back))
    ]
    return [
        s / 3.0 + 2.0 / 3.0 * (w + STEP * t) for s, w, t in zip(start, two, tendency(two, back))
    ]


def put_rows(ref, k, plane, field):
    ref[k, plane * ROWS : (plane + 1) * ROWS] = field[:ROWS]
    ref[k, OWN + plane : OWN + plane + 1] = field[2 * ROWS - 1 :]
    ref[k, OWN + PLANES + plane : OWN + PLANES + plane + 1] = field[ROWS : ROWS + 1]


def inner_kernel(ext_ref, pick_ref, weight_ref, rows_ref, strip_ref, part_ref, table_ref):
    lane = iota((2 * ROWS, COLS), 1)
    for t in range(STRIPS):
        strip = jnp.zeros((2 * ROWS, COLS), F32)
        for kk, field in enumerate(strip_fields(t)):
            plane = ext_ref[field]
            strip = jnp.where(lane >= 32 * kk + 4, roll(plane, 32 * kk + 4, 1), strip)
            strip = jnp.where(lane >= 32 * kk + 16, roll(plane, 32 * kk + 28, 1), strip)
        strip_ref[t] = strip
    rows_ref[:, OWN + 2 * PLANES :] = jnp.zeros((K, COLS - OWN - 2 * PLANES, COLS), F32)
    for level in range(L):
        base = K * PLANES + level
        back = [ext_ref[base + c * L][None] for c in range(3)]

        def body(i, carry, level=level, back=back):
            start = [
                jnp.stack(
                    [ext_ref[(i * BATCH + b) * PLANES + c * L + level] for b in range(BATCH)]
                )
                for c in range(3)
            ]
            done = advance(start, back)
            for c in range(3):
                for b in range(BATCH):
                    put_rows(rows_ref, i * BATCH + b, c * L + level, done[c][b])
            return carry

        lax.fori_loop(0, K // BATCH, body, 0)
    inner = iota((COLS, COLS), 1)
    inner = (inner >= 3) & (inner < COLS - 3)
    for k in range(K):
        put_table(table_ref, k * COLS, jnp.where(inner, rows_ref[k], 0.0).T)

    def sample(step, carry):
        at, high2, low2 = picked(pick_ref, step)
        weight = weight_ref[:, at]
        out = jnp.zeros((K, CHUNK), F32)
        sub = iota((K, CHUNK), 0)
        for k in range(K):
            part = mixed(table_ref[k * COLS : (k + 1) * COLS], high2, low2) * weight
            out = jnp.where(sub == k, jnp.sum(part, axis=0, keepdims=True), out)
        part_ref[:, at] = out
        return carry

    lax.fori_loop(0, OBS // CHUNK, sample, 0, unroll=True)


def picked(pick_ref, step):
    at = pl.ds(pl.multiple_of(step * CHUNK, CHUNK), CHUNK)
    high, low = pick_ref[0:COLS, at], pick_ref[COLS : 2 * COLS, at]
    return at, jnp.concatenate([high, high], axis=0), jnp.concatenate([low, low], axis=0)


def mixed(part, high2, low2):
    return jnp.dot(part, high2, preferred_element_type=F32) + jnp.dot(
        part, low2, preferred_element_type=F32
    )


def put_table(ref, at, value):
    high = value.astype(jnp.bfloat16)
    low = (value - high.astype(F32)).astype(jnp.bfloat16)
    ref[at : at + value.shape[0], 0:COLS] = high
    ref[at : at + value.shape[0], COLS : 2 * COLS] = low


def weights_kernel(site_ref, off_ref, err_ref, pick_ref, weight_ref, ends_ref):
    def step(i, carry):
        at = pl.ds(pl.multiple_of(i * CHUNK, CHUNK), CHUNK)
        site = site_ref[:, at]
        shift_x = off_ref[0:1, at]
        shift_y = off_ref[1:2, at]
        row_at = site // COLS
        plane = site // (ROWS * COLS)
        row = row_at % ROWS
        col = site % COLS
        size_x = jnp.abs(shift_x)
        size_y = jnp.abs(shift_y)
        before = jnp.where(row == 0, OWN + plane, row_at - 1)
        after = jnp.where(row == ROWS - 1, OWN + PLANES + plane, row_at + 1)
        beside = jnp.where(shift_x < 0.0, before, after)
        next_col = jnp.where(shift_y < 0.0, col - 1, col + 1)
        own_x = 1.0 - size_x
        scale = 1.0 / jnp.sqrt(err_ref[:, at])
        own_y = (1.0 - size_y) * scale
        side_y = size_y * scale

        def split(value):
            high = value.astype(jnp.bfloat16).astype(F32)
            return high, value - high

        own_high, own_low = split(own_x)
        side_high, side_low = split(size_x)
        index = iota((COLS, CHUNK), 0)
        at_own = index == row_at
        at_side = index == beside
        pick_high = jnp.where(at_own, own_high, jnp.where(at_side, side_high, 0.0))
        pick_low = jnp.where(at_own, own_low, jnp.where(at_side, side_low, 0.0))
        pick_ref[0:COLS, at] = pick_high.astype(jnp.bfloat16)
        pick_ref[COLS : 2 * COLS, at] = pick_low.astype(jnp.bfloat16)
        weight_ref[:, at] = jnp.where(
            index == col, own_y, jnp.where(index == next_col, side_y, 0.0)
        )
        line = iota((ROWS, CHUNK), 0)
        line = jnp.where(line < 4, line - 1, line + COLS - 7)
        ends_ref[:, at] = jnp.where(line == col, own_y, jnp.where(line == next_col, side_y, 0.0))
        return carry

    lax.fori_loop(0, OBS // CHUNK, step, 0)


def main_kernel(
    rows_ref, strip_ref, part_ref, got_one, got_two, pick_ref, ends_ref,
    bred_ref, scaled_ref, sums_ref,
    whole_ref, side_ref, edge_ref, pair_ref,
):
    at_odd_col = odd_col()
    lane = iota((2 * ROWS, COLS), 1)
    eighth = (lane & 31) // 4
    for group in range(GROUPS):
        left = jnp.where(at_odd_col, got_one[group], got_two[group])
        right = jnp.where(at_odd_col, got_two[group], got_one[group])
        for u in range(8):
            t = group * 8 + u
            if t >= STRIPS:
                break
            strip = jnp.where(eighth == 0, roll(left, 4 - 4 * u, 1), strip_ref[t])
            whole_ref[t] = jnp.where(eighth == 7, roll(right, 28 - 4 * u, 1), strip)
    side_ref[:, OWN + 2 * PLANES :] = jnp.zeros((2, COLS - OWN - 2 * PLANES, COLS), F32)
    results = []
    for level in range(L):
        mixed_back = whole_ref[2 * PLANES + level]
        back = []
        for c in range(3):
            spread_back = mixed_back
            for kk in range(4):
                if kk != c:
                    spread_back = jnp.where(
                        lane // 32 == kk, roll(mixed_back, 32 * (kk - c), 1), spread_back
                    )
            back.append(spread_back[None])
        start = [
            whole_ref[2 * (c * L + level) : 2 * (c * L + level) + 2] for c in range(3)
        ]
        results.append(advance(start, back))
    for level in range(L):
        for c in range(3):
            for half in range(2):
                put_rows(side_ref, half, c * L + level, results[level][c][half])

    across = [side_ref[half].T for half in range(2)]
    lines = []
    for k in range(K):
        turned, at = across[k // 4], 32 * (k % 4)
        lines += [turned[at + 3 : at + 7], turned[at + 25 : at + 29]]
    put_table(edge_ref, 0, jnp.concatenate(lines, axis=0))
    lane = iota((OWN, COLS), 1)
    for pair in range(0, K, 2):
        fields = []
        for k in (pair, pair + 1):
            side, kk = side_ref[k // 4, 0:OWN], k % 4
            field = jnp.where(lane < 3, roll(side, -(32 * kk + 4), 1), rows_ref[k, 0:OWN])
            fields.append(jnp.where(lane >= COLS - 3, roll(side, 100 - 32 * kk, 1), field))
        for k, field in zip((pair, pair + 1), fields):
            bred_ref[k * PLANES : (k + 1) * PLANES] = field.reshape(PLANES, ROWS, COLS)

    for i in range(K):
        mine = bred_ref[i * PLANES : (i + 1) * PLANES]
        for j in range(i, K):
            other = mine if i == j else bred_ref[j * PLANES : (j + 1) * PLANES]
            row = jnp.sum(jnp.sum(mine * other, axis=0), axis=0, keepdims=True)
            pair_ref[i * K + j : i * K + j + 1] = row
            if i != j:
                pair_ref[j * K + i : j * K + i + 1] = row
    pair_ref[K * K :] = jnp.zeros((COLS - K * K, COLS), F32)
    contract_last = (((1,), (1,)), ((), ()))
    gram_row = lax.dot_general(
        jnp.ones((8, COLS), F32), pair_ref[...], contract_last,
        precision=highest, preferred_element_type=F32,
    )[0:1]

    def sample(step, carry):
        at, high2, low2 = picked(pick_ref, step)
        ends = mixed(edge_ref[...], high2, low2)
        out = part_ref[:, at]
        sub = iota((K, CHUNK), 0)
        for k in range(K):
            part = ends[k * ROWS : (k + 1) * ROWS] * ends_ref[:, at]
            out = jnp.where(sub == k, out + jnp.sum(part, axis=0, keepdims=True), out)
        scaled_ref[:, at] = out
        return carry

    lax.fori_loop(0, OBS // CHUNK, sample, 0, unroll=True)

    scaled = scaled_ref[...]
    normal = lax.dot_general(
        scaled, scaled, contract_last, precision=highest, preferred_element_type=F32
    )
    row = gram_row
    wide = jnp.concatenate([normal, jnp.zeros((K, COLS - K), F32)], axis=1)
    for i in range(K):
        row = row + roll(wide[i : i + 1], K * K + K * i, 1)
    sums_ref[...] = row


def inverse_of_factor(a):
    n = len(a)
    low = [[None] * n for _ in range(n)]
    inv = [[None] * n for _ in range(n)]
    for j in range(n):
        total = a[j][j]
        for k in range(j):
            total = total - low[j][k] * low[j][k]
        root = jnp.sqrt(total)
        inv[j][j] = 1.0 / root
        for i in range(j + 1, n):
            total = a[i][j]
            for k in range(j):
                total = total - low[i][k] * low[j][k]
            low[i][j] = total * inv[j][j]
    for j in range(n):
        for i in range(j + 1, n):
            total = low[i][j] * inv[j][j]
            for k in range(j + 1, i):
                total = total + low[i][k] * inv[k][j]
            inv[i][j] = -total * inv[i][i]
    return inv


def added(terms):
    total = terms[0]
    for term in terms[1:]:
        total = total + term
    return total


def final_kernel(cells_all, obs_all, sums_ref, bred_ref, scaled_ref, analysis_ref, perturb_ref):
    row = sums_ref[...]
    tile = (ROWS, COLS)

    def entry(at):
        return jnp.broadcast_to(row[:, at : at + 1], tile)

    gram = [[entry(i * K + j) / cells_all if j <= i else None for j in range(K)] for i in range(K)]
    normal = [[None] * K for _ in range(K)]
    for i in range(K):
        for j in range(i + 1):
            normal[i][j] = normal[j][i] = entry(K * K + i * K + j) / obs_all
    inv_lower = inverse_of_factor(gram)
    half = [
        [added([inv_lower[i][k] * normal[k][j] for k in range(i + 1)]) for j in range(K)]
        for i in range(K)
    ]
    system = [
        [
            added([half[i][k] * inv_lower[j][k] for k in range(j + 1)]) + (1.0 if i == j else 0.0)
            for j in range(i + 1)
        ]
        for i in range(K)
    ]
    inv_factor = inverse_of_factor(system)
    combo = [
        [added([inv_factor[i][k] * inv_lower[k][j] for k in range(j, i + 1)]) for j in range(i + 1)]
        for i in range(K)
    ]
    for plane in range(PLANES):
        fields = [bred_ref[j * PLANES + plane] for j in range(K)]
        for k in range(K):
            analysis_ref[k * PLANES + plane] = added(
                [combo[k][j] * fields[j] for j in range(k + 1)]
            )
    sub = iota(tile, 0)
    columns = []
    for j in range(K):
        column = jnp.zeros(tile, F32)
        for k in range(j, K):
            column = jnp.where(sub == k, combo[k][j], column)
        columns.append(column)
    for at in range(0, OBS, COLS):
        part = scaled_ref[:, at : at + COLS]
        perturb_ref[:, at : at + COLS] = added(
            [columns[j] * part[j : j + 1] for j in range(K)]
        )


def shape(*dims):
    return jax.ShapeDtypeStruct(dims, F32)


def swap(packed, axes):
    count = lax.axis_size(axes)
    first = [(i, i ^ 1) for i in range(count)]
    second = [((i - 1) % count, ((i ^ 1) - 1) % count) for i in range(count)]
    far = lax.ppermute(packed[1], axes, second)
    near = lax.ppermute(packed[0], axes, first)
    return near, far


def small(mib):
    return pltpu.CompilerParams(vmem_limit_bytes=mib << 20)


def spread(row, axes):
    count = lax.axis_size(axes)
    copies = jnp.broadcast_to(row[None], (count, 1, COLS))
    return lax.all_to_all(copies, axes, 0, 0, tiled=True).sum(axis=0)


def main_call(*operands):
    return pl.pallas_call(
        main_kernel,
        out_shape=(shape(K * PLANES, ROWS, COLS), shape(K, OBS), shape(1, COLS)),
        scratch_shapes=[
            pltpu.VMEM((STRIPS, 2 * ROWS, COLS), F32),
            pltpu.VMEM((2, COLS, COLS), F32),
            pltpu.VMEM((K * ROWS, 2 * COLS), jnp.bfloat16),
            pltpu.VMEM((COLS, COLS), F32),
        ],
        compiler_params=small(16),
        name="edges",
    )(*operands)


def busy(us):
    return pl.CostEstimate(flops=us * 10**9, bytes_accessed=0, transcendentals=0)


def local(vectors, background, obs_site, obs_offset, obs_error):
    devices_all = lax.axis_size(GX) * lax.axis_size(GY)
    cells_all = float(PLANES * ROWS * COLS * devices_all)
    obs_all = float(OBS * devices_all)
    vec = vectors.reshape(K * PLANES, ROWS, COLS)
    back = background.reshape(PLANES, ROWS, COLS)
    own, *packed = pl.pallas_call(
        pack_rows_kernel,
        out_shape=(shape(FIELDS, ROWS, COLS),) + (shape(HALF, ROWS, COLS),) * 2,
        compiler_params=small(8),
        name="pack_rows",
    )(vec, back)
    got = swap(packed, GX)
    weights = pl.pallas_call(
        weights_kernel,
        out_shape=(
            jax.ShapeDtypeStruct((2 * COLS, OBS), jnp.bfloat16), shape(COLS, OBS), shape(ROWS, OBS)
        ),
        compiler_params=small(8),
        cost_estimate=busy(3),
        name="weights",
    )(obs_site.reshape(1, OBS), obs_offset, obs_error.reshape(1, OBS))
    ext, *packed = pl.pallas_call(
        pack_cols_kernel,
        out_shape=(shape(FIELDS, 2 * ROWS, COLS),) + (shape(GROUPS, 2 * ROWS, COLS),) * 2,
        compiler_params=small(8),
        name="pack_cols",
    )(own, *got)
    got = swap(packed, GY)
    pick, weight, ends = weights
    mine = pl.pallas_call(
        inner_kernel,
        out_shape=(shape(K, COLS, COLS), shape(STRIPS, 2 * ROWS, COLS), shape(K, OBS)),
        scratch_shapes=[pltpu.VMEM((K * COLS, 2 * COLS), jnp.bfloat16)],
        compiler_params=small(16),
        cost_estimate=busy(8),
        name="inner",
    )(ext, pick, weight)
    bred, scaled, sums = main_call(*mine, *got, pick, ends)
    sums = spread(spread(sums, FLAT), DEEP)
    analysis, perturb = pl.pallas_call(
        functools.partial(final_kernel, cells_all, obs_all),
        out_shape=(shape(K * PLANES, ROWS, COLS), shape(K, OBS)),
        compiler_params=small(8),
        name="combine",
    )(sums, bred, scaled)
    return (analysis.reshape(vectors.shape), perturb)


def solution(mesh):
    torus = Mesh(mesh.devices.reshape(8, 4, 2, 4, 2), GX_GY)
    return jax.shard_map(
        local,
        mesh=torus,
        in_specs=(
            P(None, None, None, GX, GY),
            P(None, None, GX, GY),
            P(GX_GY),
            P(None, GX_GY),
            P(GX_GY),
        ),
        out_specs=(P(None, None, None, GX, GY), P(None, GX_GY)),
        check_vma=False,
    )
```

```python
import functools

import jax
import jax.numpy as jnp
from jax import lax
from jax.experimental import pallas as pl
from jax.experimental.pallas import tpu as pltpu
from jax.sharding import Mesh
from jax.sharding import PartitionSpec as P

K = 8
L = 4
PLANES = 3 * L
ROWS = 8
COLS = 128
OBS = 4096
GX = ("z_lo", "y")
GY = ("z_hi", "x", "core")
GX_GY = GX + GY
FLAT = ("y", "x", "core")
DEEP = ("z_lo", "z_hi")
FIELDS = K * PLANES + PLANES
HALF = FIELDS // 2
GROUPS = 4
STRIPS = 2 * PLANES + L
CHUNK = 512
BATCH = 4
OWN = PLANES * ROWS
STEP = 0.35
F32 = jnp.float32
highest = lax.Precision.HIGHEST


def iota(shape, dim):
    return lax.broadcasted_iota(jnp.int32, shape, dim)


def roll(x, shift, axis):
    axis = axis % x.ndim
    shift = shift % x.shape[axis]
    return x if shift == 0 else pltpu.roll(x, shift, axis)


def odd_row():
    return lax.rem(lax.axis_index("y"), 2) == 1


def odd_col():
    return lax.axis_index("core") == 1


def pack_rows_kernel(own_ref, one_ref, two_ref):
    odd = odd_row()
    first = own_ref[0:HALF]
    second = roll(own_ref[HALF:FIELDS], 4, 1)
    top = iota((HALF, ROWS, COLS), 1) < 4
    down = jnp.where(top, first, second)
    up = jnp.where(top, second, first)
    one_ref[...] = jnp.where(odd, down, up)
    two_ref[...] = jnp.where(odd, up, down)


def pack_cols_kernel(own_ref, got_one, got_two, ext_ref, one_ref, two_ref):
    at_odd_row = odd_row()
    at_odd_col = odd_col()
    ext_ref[:, 0:ROWS] = own_ref[...]
    top = iota((HALF, ROWS, COLS), 1) < 4
    low = jnp.where(at_odd_row, got_one[...], got_two[...])
    high = jnp.where(at_odd_row, got_two[...], got_one[...])
    ext_ref[0:HALF, ROWS : 2 * ROWS] = jnp.where(top, high, low)
    ext_ref[HALF:FIELDS, ROWS : 2 * ROWS] = roll(jnp.where(top, low, high), 4, 1)
    lane = iota((2 * ROWS, COLS), 1)
    for group in range(GROUPS):
        up = jnp.zeros((2 * ROWS, COLS), F32)
        down = jnp.zeros((2 * ROWS, COLS), F32)
        for u in range(min(8, STRIPS - group * 8)):
            for kk, field in enumerate(strip_fields(group * 8 + u)):
                moved = roll(ext_ref[field], 32 * kk + 4 * u, 1)
                down = jnp.where(lane // 4 == 8 * kk + u, moved, down)
                up = jnp.where(lane // 4 == (8 * kk + u + 31) % 32, moved, up)
        one_ref[group] = jnp.where(at_odd_col, down, up)
        two_ref[group] = jnp.where(at_odd_col, up, down)


def strip_fields(t):
    if t < 2 * PLANES:
        plane, half = t // 2, t % 2
        return [(half * 4 + kk) * PLANES + plane for kk in range(4)]
    return [K * PLANES + c * L + t - 2 * PLANES for c in range(3)]


def tendency(state, back):
    wind_x, wind_y, vort = back
    east, north, height = state

    def along_x(f):
        return 0.5 * (roll(f, -1, f.ndim - 2) - roll(f, 1, f.ndim - 2))

    def along_y(f):
        return 0.5 * (roll(f, -1, f.ndim - 1) - roll(f, 1, f.ndim - 1))

    ex, nx, hx = along_x(east), along_x(north), along_x(height)
    ey, ny, hy = along_y(east), along_y(north), along_y(height)
    tend_east = -(wind_x * ex + wind_y * ey) - hx + vort * north
    tend_north = -(wind_x * nx + wind_y * ny) - hy - vort * east
    tend_height = -(wind_x * hx + wind_y * hy) - (ex + ny)
    return tend_east, tend_north, tend_height


def advance(start, back):
    one = [s + STEP * t for s, t in zip(start, tendency(start, back))]
    two = [
        0.75 * s + 0.25 * (o + STEP * t) for s, o, t in zip(start, one, tendency(one, back))
    ]
    return [
        s / 3.0 + 2.0 / 3.0 * (w + STEP * t) for s, w, t in zip(start, two, tendency(two, back))
    ]


def put_rows(ref, k, plane, field):
    ref[k, plane * ROWS : (plane + 1) * ROWS] = field[:ROWS]
    ref[k, OWN + plane : OWN + plane + 1] = field[2 * ROWS - 1 :]
    ref[k, OWN + PLANES + plane : OWN + PLANES + plane + 1] = field[ROWS : ROWS + 1]


def inner_kernel(ext_ref, pick_ref, weight_ref, rows_ref, strip_ref, part_ref, table_ref):
    lane = iota((2 * ROWS, COLS), 1)
    for t in range(STRIPS):
        strip = jnp.zeros((2 * ROWS, COLS), F32)
        for kk, field in enumerate(strip_fields(t)):
            plane = ext_ref[field]
            strip = jnp.where(lane >= 32 * kk + 4, roll(plane, 32 * kk + 4, 1), strip)
            strip = jnp.where(lane >= 32 * kk + 16, roll(plane, 32 * kk + 28, 1), strip)
        strip_ref[t] = strip
    rows_ref[:, OWN + 2 * PLANES :] = jnp.zeros((K, COLS - OWN - 2 * PLANES, COLS), F32)
    for level in range(L):
        base = K * PLANES + level
        back = [ext_ref[base + c * L][None] for c in range(3)]

        def body(i, carry, level=level, back=back):
            start = [
                jnp.stack(
                    [ext_ref[(i * BATCH + b) * PLANES + c * L + level] for b in range(BATCH)]
                )
                for c in range(3)
            ]
            done = advance(start, back)
            for c in range(3):
                for b in range(BATCH):
                    put_rows(rows_ref, i * BATCH + b, c * L + level, done[c][b])
            return carry

        lax.fori_loop(0, K // BATCH, body, 0)
    inner = iota((COLS, COLS), 1)
    inner = (inner >= 3) & (inner < COLS - 3)
    for k in range(K):
        put_table(table_ref, k * COLS, jnp.where(inner, rows_ref[k], 0.0).T)

    def sample(step, carry):
        at, high2, low2 = picked(pick_ref, step)
        weight = weight_ref[:, at]
        out = jnp.zeros((K, CHUNK), F32)
        sub = iota((K, CHUNK), 0)
        for k in range(K):
            part = mixed(table_ref[k * COLS : (k + 1) * COLS], high2, low2) * weight
            out = jnp.where(sub == k, jnp.sum(part, axis=0, keepdims=True), out)
        part_ref[:, at] = out
        return carry

    lax.fori_loop(0, OBS // CHUNK, sample, 0, unroll=True)


def picked(pick_ref, step):
    at = pl.ds(pl.multiple_of(step * CHUNK, CHUNK), CHUNK)
    high, low = pick_ref[0:COLS, at], pick_ref[COLS : 2 * COLS, at]
    return at, jnp.concatenate([high, high], axis=0), jnp.concatenate([low, low], axis=0)


def mixed(part, high2, low2):
    return jnp.dot(part, high2, preferred_element_type=F32) + jnp.dot(
        part, low2, preferred_element_type=F32
    )


def put_table(ref, at, value):
    high = value.astype(jnp.bfloat16)
    low = (value - high.astype(F32)).astype(jnp.bfloat16)
    ref[at : at + value.shape[0], 0:COLS] = high
    ref[at : at + value.shape[0], COLS : 2 * COLS] = low


def weights_kernel(site_ref, off_ref, err_ref, pick_ref, weight_ref, ends_ref):
    def step(i, carry):
        at = pl.ds(pl.multiple_of(i * CHUNK, CHUNK), CHUNK)
        site = site_ref[:, at]
        shift_x = off_ref[0:1, at]
        shift_y = off_ref[1:2, at]
        row_at = site // COLS
        plane = site // (ROWS * COLS)
        row = row_at % ROWS
        col = site % COLS
        size_x = jnp.abs(shift_x)
        size_y = jnp.abs(shift_y)
        before = jnp.where(row == 0, OWN + plane, row_at - 1)
        after = jnp.where(row == ROWS - 1, OWN + PLANES + plane, row_at + 1)
        beside = jnp.where(shift_x < 0.0, before, after)
        next_col = jnp.where(shift_y < 0.0, col - 1, col + 1)
        own_x = 1.0 - size_x
        scale = 1.0 / jnp.sqrt(err_ref[:, at])
        own_y = (1.0 - size_y) * scale
        side_y = size_y * scale

        def split(value):
            high = value.astype(jnp.bfloat16).astype(F32)
            return high, value - high

        own_high, own_low = split(own_x)
        side_high, side_low = split(size_x)
        index = iota((COLS, CHUNK), 0)
        at_own = index == row_at
        at_side = index == beside
        pick_high = jnp.where(at_own, own_high, jnp.where(at_side, side_high, 0.0))
        pick_low = jnp.where(at_own, own_low, jnp.where(at_side, side_low, 0.0))
        pick_ref[0:COLS, at] = pick_high.astype(jnp.bfloat16)
        pick_ref[COLS : 2 * COLS, at] = pick_low.astype(jnp.bfloat16)
        weight_ref[:, at] = jnp.where(
            index == col, own_y, jnp.where(index == next_col, side_y, 0.0)
        )
        line = iota((ROWS, CHUNK), 0)
        line = jnp.where(line < 4, line - 1, line + COLS - 7)
        ends_ref[:, at] = jnp.where(line == col, own_y, jnp.where(line == next_col, side_y, 0.0))
        return carry

    lax.fori_loop(0, OBS // CHUNK, step, 0)


def main_kernel(
    rows_ref, strip_ref, part_ref, got_one, got_two, pick_ref, ends_ref,
    bred_ref, scaled_ref, sums_ref,
    whole_ref, side_ref, edge_ref, pair_ref,
):
    at_odd_col = odd_col()
    lane = iota((2 * ROWS, COLS), 1)
    eighth = (lane & 31) // 4
    for group in range(GROUPS):
        left = jnp.where(at_odd_col, got_one[group], got_two[group])
        right = jnp.where(at_odd_col, got_two[group], got_one[group])
        for u in range(8):
            t = group * 8 + u
            if t >= STRIPS:
                break
            strip = jnp.where(eighth == 0, roll(left, 4 - 4 * u, 1), strip_ref[t])
            whole_ref[t] = jnp.where(eighth == 7, roll(right, 28 - 4 * u, 1), strip)
    side_ref[:, OWN + 2 * PLANES :] = jnp.zeros((2, COLS - OWN - 2 * PLANES, COLS), F32)
    results = []
    for level in range(L):
        mixed_back = whole_ref[2 * PLANES + level]
        back = []
        for c in range(3):
            spread_back = mixed_back
            for kk in range(4):
                if kk != c:
                    spread_back = jnp.where(
                        lane // 32 == kk, roll(mixed_back, 32 * (kk - c), 1), spread_back
                    )
            back.append(spread_back[None])
        start = [
            whole_ref[2 * (c * L + level) : 2 * (c * L + level) + 2] for c in range(3)
        ]
        results.append(advance(start, back))
    for level in range(L):
        for c in range(3):
            for half in range(2):
                put_rows(side_ref, half, c * L + level, results[level][c][half])

    across = [side_ref[half].T for half in range(2)]
    lines = []
    for k in range(K):
        turned, at = across[k // 4], 32 * (k % 4)
        lines += [turned[at + 3 : at + 7], turned[at + 25 : at + 29]]
    put_table(edge_ref, 0, jnp.concatenate(lines, axis=0))
    lane = iota((OWN, COLS), 1)
    for pair in range(0, K, 2):
        fields = []
        for k in (pair, pair + 1):
            side, kk = side_ref[k // 4, 0:OWN], k % 4
            field = jnp.where(lane < 3, roll(side, -(32 * kk + 4), 1), rows_ref[k, 0:OWN])
            fields.append(jnp.where(lane >= COLS - 3, roll(side, 100 - 32 * kk, 1), field))
        for k, field in zip((pair, pair + 1), fields):
            bred_ref[k * PLANES : (k + 1) * PLANES] = field.reshape(PLANES, ROWS, COLS)

    for i in range(K):
        mine = bred_ref[i * PLANES : (i + 1) * PLANES]
        for j in range(i, K):
            other = mine if i == j else bred_ref[j * PLANES : (j + 1) * PLANES]
            row = jnp.sum(jnp.sum(mine * other, axis=0), axis=0, keepdims=True)
            pair_ref[i * K + j : i * K + j + 1] = row
            if i != j:
                pair_ref[j * K + i : j * K + i + 1] = row
    pair_ref[K * K :] = jnp.zeros((COLS - K * K, COLS), F32)
    contract_last = (((1,), (1,)), ((), ()))
    gram_row = lax.dot_general(
        jnp.ones((8, COLS), F32), pair_ref[...], contract_last,
        precision=highest, preferred_element_type=F32,
    )[0:1]

    def sample(step, carry):
        at, high2, low2 = picked(pick_ref, step)
        ends = mixed(edge_ref[...], high2, low2)
        out = part_ref[:, at]
        sub = iota((K, CHUNK), 0)
        for k in range(K):
            part = ends[k * ROWS : (k + 1) * ROWS] * ends_ref[:, at]
            out = jnp.where(sub == k, out + jnp.sum(part, axis=0, keepdims=True), out)
        scaled_ref[:, at] = out
        return carry

    lax.fori_loop(0, OBS // CHUNK, sample, 0, unroll=True)

    scaled = scaled_ref[...]
    normal = lax.dot_general(
        scaled, scaled, contract_last, precision=highest, preferred_element_type=F32
    )
    row = gram_row
    wide = jnp.concatenate([normal, jnp.zeros((K, COLS - K), F32)], axis=1)
    for i in range(K):
        row = row + roll(wide[i : i + 1], K * K + K * i, 1)
    sums_ref[...] = row


def inverse_of_factor(a):
    n = len(a)
    low = [[None] * n for _ in range(n)]
    inv = [[None] * n for _ in range(n)]
    for j in range(n):
        total = a[j][j]
        for k in range(j):
            total = total - low[j][k] * low[j][k]
        root = jnp.sqrt(total)
        inv[j][j] = 1.0 / root
        for i in range(j + 1, n):
            total = a[i][j]
            for k in range(j):
                total = total - low[i][k] * low[j][k]
            low[i][j] = total * inv[j][j]
    for j in range(n):
        for i in range(j + 1, n):
            total = low[i][j] * inv[j][j]
            for k in range(j + 1, i):
                total = total + low[i][k] * inv[k][j]
            inv[i][j] = -total * inv[i][i]
    return inv


def added(terms):
    total = terms[0]
    for term in terms[1:]:
        total = total + term
    return total


def final_kernel(cells_all, obs_all, sums_ref, bred_ref, scaled_ref, analysis_ref, perturb_ref):
    row = sums_ref[...]
    tile = (ROWS, COLS)

    def entry(at):
        return jnp.broadcast_to(row[:, at : at + 1], tile)

    gram = [[entry(i * K + j) / cells_all if j <= i else None for j in range(K)] for i in range(K)]
    normal = [[None] * K for _ in range(K)]
    for i in range(K):
        for j in range(i + 1):
            normal[i][j] = normal[j][i] = entry(K * K + i * K + j) / obs_all
    inv_lower = inverse_of_factor(gram)
    half = [
        [added([inv_lower[i][k] * normal[k][j] for k in range(i + 1)]) for j in range(K)]
        for i in range(K)
    ]
    system = [
        [
            added([half[i][k] * inv_lower[j][k] for k in range(j + 1)]) + (1.0 if i == j else 0.0)
            for j in range(i + 1)
        ]
        for i in range(K)
    ]
    inv_factor = inverse_of_factor(system)
    combo = [
        [added([inv_factor[i][k] * inv_lower[k][j] for k in range(j, i + 1)]) for j in range(i + 1)]
        for i in range(K)
    ]
    for plane in range(PLANES):
        fields = [bred_ref[j * PLANES + plane] for j in range(K)]
        for k in range(K):
            analysis_ref[k * PLANES + plane] = added(
                [combo[k][j] * fields[j] for j in range(k + 1)]
            )
    sub = iota(tile, 0)
    columns = []
    for j in range(K):
        column = jnp.zeros(tile, F32)
        for k in range(j, K):
            column = jnp.where(sub == k, combo[k][j], column)
        columns.append(column)
    for at in range(0, OBS, COLS):
        part = scaled_ref[:, at : at + COLS]
        perturb_ref[:, at : at + COLS] = added(
            [columns[j] * part[j : j + 1] for j in range(K)]
        )


def shape(*dims):
    return jax.ShapeDtypeStruct(dims, F32)


def swap(packed, axes):
    count = lax.axis_size(axes)
    first = [(i, i ^ 1) for i in range(count)]
    second = [((i - 1) % count, ((i ^ 1) - 1) % count) for i in range(count)]
    far = lax.ppermute(packed[1], axes, second)
    near = lax.ppermute(packed[0], axes, first)
    return near, far


def small(mib):
    return pltpu.CompilerParams(vmem_limit_bytes=mib << 20)


def spread(row, axes):
    count = lax.axis_size(axes)
    copies = jnp.broadcast_to(row[None], (count, 1, COLS))
    return lax.all_to_all(copies, axes, 0, 0, tiled=True).sum(axis=0)


def main_call(*operands):
    return pl.pallas_call(
        main_kernel,
        out_shape=(shape(K * PLANES, ROWS, COLS), shape(K, OBS), shape(1, COLS)),
        scratch_shapes=[
            pltpu.VMEM((STRIPS, 2 * ROWS, COLS), F32),
            pltpu.VMEM((2, COLS, COLS), F32),
            pltpu.VMEM((K * ROWS, 2 * COLS), jnp.bfloat16),
            pltpu.VMEM((COLS, COLS), F32),
        ],
        compiler_params=small(16),
        name="edges",
    )(*operands)


def busy(us):
    return pl.CostEstimate(flops=us * 10**9, bytes_accessed=0, transcendentals=0)


def local(vectors, background, obs_site, obs_offset, obs_error):
    devices_all = lax.axis_size(GX) * lax.axis_size(GY)
    cells_all = float(PLANES * ROWS * COLS * devices_all)
    obs_all = float(OBS * devices_all)
    vec = vectors.reshape(K * PLANES, ROWS, COLS)
    back = background.reshape(PLANES, ROWS, COLS)
    own = jnp.concatenate([vec, back], axis=0)
    packed = pl.pallas_call(
        pack_rows_kernel,
        out_shape=(shape(HALF, ROWS, COLS),) * 2,
        compiler_params=small(8),
        name="pack_rows",
    )(own)
    got = swap(packed, GX)
    weights = pl.pallas_call(
        weights_kernel,
        out_shape=(
            jax.ShapeDtypeStruct((2 * COLS, OBS), jnp.bfloat16), shape(COLS, OBS), shape(ROWS, OBS)
        ),
        compiler_params=small(8),
        cost_estimate=busy(3),
        name="weights",
    )(obs_site.reshape(1, OBS), obs_offset, obs_error.reshape(1, OBS))
    ext, *packed = pl.pallas_call(
        pack_cols_kernel,
        out_shape=(shape(FIELDS, 2 * ROWS, COLS),) + (shape(GROUPS, 2 * ROWS, COLS),) * 2,
        compiler_params=small(8),
        name="pack_cols",
    )(own, *got)
    got = swap(packed, GY)
    pick, weight, ends = weights
    mine = pl.pallas_call(
        inner_kernel,
        out_shape=(shape(K, COLS, COLS), shape(STRIPS, 2 * ROWS, COLS), shape(K, OBS)),
        scratch_shapes=[pltpu.VMEM((K * COLS, 2 * COLS), jnp.bfloat16)],
        compiler_params=small(16),
        cost_estimate=busy(8),
        name="inner",
    )(ext, pick, weight)
    bred, scaled, sums = main_call(*mine, *got, pick, ends)
    sums = spread(spread(sums, FLAT), DEEP)
    analysis, perturb = pl.pallas_call(
        functools.partial(final_kernel, cells_all, obs_all),
        out_shape=(shape(K * PLANES, ROWS, COLS), shape(K, OBS)),
        compiler_params=small(8),
        name="combine",
    )(sums, bred, scaled)
    return (analysis.reshape(vectors.shape), perturb)


def solution(mesh):
    torus = Mesh(mesh.devices.reshape(8, 4, 2, 4, 2), GX_GY)
    return jax.shard_map(
        local,
        mesh=torus,
        in_specs=(
            P(None, None, None, GX, GY),
            P(None, None, GX, GY),
            P(GX_GY),
            P(None, GX_GY),
            P(GX_GY),
        ),
        out_specs=(P(None, None, None, GX, GY), P(None, GX_GY)),
        check_vma=False,
    )
```

```python
import functools

import jax
import jax.numpy as jnp
from jax import lax
from jax.experimental import pallas as pl
from jax.experimental.pallas import tpu as pltpu
from jax.sharding import Mesh
from jax.sharding import PartitionSpec as P

K = 8
L = 4
PLANES = 3 * L
ROWS = 8
COLS = 128
OBS = 4096
GX = ("z_lo", "y")
GY = ("z_hi", "x", "core")
GX_GY = GX + GY
FLAT = ("y", "x", "core")
DEEP = ("z_lo", "z_hi")
FIELDS = K * PLANES + PLANES
HALF = FIELDS // 2
GROUPS = 4
STRIPS = 2 * PLANES + L
CHUNK = 512
BATCH = 4
OWN = PLANES * ROWS
STEP = 0.35
F32 = jnp.float32
highest = lax.Precision.HIGHEST


def iota(shape, dim):
    return lax.broadcasted_iota(jnp.int32, shape, dim)


def roll(x, shift, axis):
    axis = axis % x.ndim
    shift = shift % x.shape[axis]
    return x if shift == 0 else pltpu.roll(x, shift, axis)


def odd_row():
    return lax.rem(lax.axis_index("y"), 2) == 1


def odd_col():
    return lax.axis_index("core") == 1


def pack_rows_kernel(own_ref, one_ref, two_ref):
    odd = odd_row()
    first = own_ref[0:HALF]
    second = roll(own_ref[HALF:FIELDS], 4, 1)
    top = iota((HALF, ROWS, COLS), 1) < 4
    down = jnp.where(top, first, second)
    up = jnp.where(top, second, first)
    one_ref[...] = jnp.where(odd, down, up)
    two_ref[...] = jnp.where(odd, up, down)


def pack_cols_kernel(own_ref, got_one, got_two, ext_ref, one_ref, two_ref):
    at_odd_row = odd_row()
    at_odd_col = odd_col()
    ext_ref[:, 0:ROWS] = own_ref[...]
    top = iota((HALF, ROWS, COLS), 1) < 4
    low = jnp.where(at_odd_row, got_one[...], got_two[...])
    high = jnp.where(at_odd_row, got_two[...], got_one[...])
    ext_ref[0:HALF, ROWS : 2 * ROWS] = jnp.where(top, high, low)
    ext_ref[HALF:FIELDS, ROWS : 2 * ROWS] = roll(jnp.where(top, low, high), 4, 1)
    lane = iota((2 * ROWS, COLS), 1)
    for group in range(GROUPS):
        up = jnp.zeros((2 * ROWS, COLS), F32)
        down = jnp.zeros((2 * ROWS, COLS), F32)
        for u in range(min(8, STRIPS - group * 8)):
            for kk, field in enumerate(strip_fields(group * 8 + u)):
                moved = roll(ext_ref[field], 32 * kk + 4 * u, 1)
                down = jnp.where(lane // 4 == 8 * kk + u, moved, down)
                up = jnp.where(lane // 4 == (8 * kk + u + 31) % 32, moved, up)
        one_ref[group] = jnp.where(at_odd_col, down, up)
        two_ref[group] = jnp.where(at_odd_col, up, down)


def strip_fields(t):
    if t < 2 * PLANES:
        plane, half = t // 2, t % 2
        return [(half * 4 + kk) * PLANES + plane for kk in range(4)]
    return [K * PLANES + c * L + t - 2 * PLANES for c in range(3)]


def tendency(state, back):
    wind_x, wind_y, vort = back
    east, north, height = state

    def along_x(f):
        return 0.5 * (roll(f, -1, f.ndim - 2) - roll(f, 1, f.ndim - 2))

    def along_y(f):
        return 0.5 * (roll(f, -1, f.ndim - 1) - roll(f, 1, f.ndim - 1))

    ex, nx, hx = along_x(east), along_x(north), along_x(height)
    ey, ny, hy = along_y(east), along_y(north), along_y(height)
    tend_east = -(wind_x * ex + wind_y * ey) - hx + vort * north
    tend_north = -(wind_x * nx + wind_y * ny) - hy - vort * east
    tend_height = -(wind_x * hx + wind_y * hy) - (ex + ny)
    return tend_east, tend_north, tend_height


def advance(start, back):
    one = [s + STEP * t for s, t in zip(start, tendency(start, back))]
    two = [
        0.75 * s + 0.25 * (o + STEP * t) for s, o, t in zip(start, one, tendency(one, back))
    ]
    return [
        s / 3.0 + 2.0 / 3.0 * (w + STEP * t) for s, w, t in zip(start, two, tendency(two, back))
    ]


def put_rows(ref, k, plane, field):
    ref[k, plane * ROWS : (plane + 1) * ROWS] = field[:ROWS]
    ref[k, OWN + plane : OWN + plane + 1] = field[2 * ROWS - 1 :]
    ref[k, OWN + PLANES + plane : OWN + PLANES + plane + 1] = field[ROWS : ROWS + 1]


def put_strips(strip_ref, tile_of):
    lane = iota((ROWS, COLS), 1)
    for t in range(STRIPS):
        strip = jnp.zeros((ROWS, COLS), F32)
        for kk, field in enumerate(strip_fields(t)):
            tile = tile_of(field)
            strip = jnp.where(lane >= 32 * kk + 4, roll(tile, 32 * kk + 4, 1), strip)
            strip = jnp.where(lane >= 32 * kk + 16, roll(tile, 32 * kk + 28, 1), strip)
        strip_ref[t] = strip


def inner_kernel(ext_ref, pick_ref, weight_ref, rows_ref, strip_ref, part_ref, table_ref):
    put_strips(strip_ref, lambda field: ext_ref[field, ROWS : 2 * ROWS])
    rows_ref[:, OWN + 2 * PLANES :] = jnp.zeros((K, COLS - OWN - 2 * PLANES, COLS), F32)
    for level in range(L):
        base = K * PLANES + level
        back = [ext_ref[base + c * L][None] for c in range(3)]

        def body(i, carry, level=level, back=back):
            start = [
                jnp.stack(
                    [ext_ref[(i * BATCH + b) * PLANES + c * L + level] for b in range(BATCH)]
                )
                for c in range(3)
            ]
            done = advance(start, back)
            for c in range(3):
                for b in range(BATCH):
                    put_rows(rows_ref, i * BATCH + b, c * L + level, done[c][b])
            return carry

        lax.fori_loop(0, K // BATCH, body, 0, unroll=True)
    inner = iota((COLS, COLS), 1)
    inner = (inner >= 3) & (inner < COLS - 3)
    for k in range(K):
        put_table(table_ref, k * COLS, jnp.where(inner, rows_ref[k], 0.0).T)

    def sample(step, carry):
        at, high2, low2 = picked(pick_ref, step)
        weight = weight_ref[:, at]
        out = jnp.zeros((K, CHUNK), F32)
        sub = iota((K, CHUNK), 0)
        for k in range(K):
            part = mixed(table_ref[k * COLS : (k + 1) * COLS], high2, low2) * weight
            out = jnp.where(sub == k, jnp.sum(part, axis=0, keepdims=True), out)
        part_ref[:, at] = out
        return carry

    lax.fori_loop(0, OBS // CHUNK, sample, 0, unroll=True)


def picked(pick_ref, step):
    at = pl.ds(pl.multiple_of(step * CHUNK, CHUNK), CHUNK)
    high, low = pick_ref[0:COLS, at], pick_ref[COLS : 2 * COLS, at]
    return at, jnp.concatenate([high, high], axis=0), jnp.concatenate([low, low], axis=0)


def mixed(part, high2, low2):
    return jnp.dot(part, high2, preferred_element_type=F32) + jnp.dot(
        part, low2, preferred_element_type=F32
    )


def put_table(ref, at, value):
    high = value.astype(jnp.bfloat16)
    low = (value - high.astype(F32)).astype(jnp.bfloat16)
    ref[at : at + value.shape[0], 0:COLS] = high
    ref[at : at + value.shape[0], COLS : 2 * COLS] = low


def weights_kernel(
    site_ref, off_ref, err_ref, own_ref, pick_ref, weight_ref, ends_ref, strip_ref
):
    put_strips(strip_ref, lambda field: own_ref[field])

    def step(i, carry):
        at = pl.ds(pl.multiple_of(i * CHUNK, CHUNK), CHUNK)
        site = site_ref[:, at]
        shift_x = off_ref[0:1, at]
        shift_y = off_ref[1:2, at]
        row_at = site // COLS
        plane = site // (ROWS * COLS)
        row = row_at % ROWS
        col = site % COLS
        size_x = jnp.abs(shift_x)
        size_y = jnp.abs(shift_y)
        before = jnp.where(row == 0, OWN + plane, row_at - 1)
        after = jnp.where(row == ROWS - 1, OWN + PLANES + plane, row_at + 1)
        beside = jnp.where(shift_x < 0.0, before, after)
        next_col = jnp.where(shift_y < 0.0, col - 1, col + 1)
        own_x = 1.0 - size_x
        scale = 1.0 / jnp.sqrt(err_ref[:, at])
        own_y = (1.0 - size_y) * scale
        side_y = size_y * scale

        def split(value):
            high = value.astype(jnp.bfloat16).astype(F32)
            return high, value - high

        own_high, own_low = split(own_x)
        side_high, side_low = split(size_x)
        index = iota((COLS, CHUNK), 0)
        at_own = index == row_at
        at_side = index == beside
        pick_high = jnp.where(at_own, own_high, jnp.where(at_side, side_high, 0.0))
        pick_low = jnp.where(at_own, own_low, jnp.where(at_side, side_low, 0.0))
        pick_ref[0:COLS, at] = pick_high.astype(jnp.bfloat16)
        pick_ref[COLS : 2 * COLS, at] = pick_low.astype(jnp.bfloat16)
        weight_ref[:, at] = jnp.where(
            index == col, own_y, jnp.where(index == next_col, side_y, 0.0)
        )
        line = iota((ROWS, CHUNK), 0)
        line = jnp.where(line < 4, line - 1, line + COLS - 7)
        ends_ref[:, at] = jnp.where(line == col, own_y, jnp.where(line == next_col, side_y, 0.0))
        return carry

    lax.fori_loop(0, OBS // CHUNK, step, 0)


def main_kernel(
    own_ref, rows_ref, strip_ref, part_ref, got_one, got_two, pick_ref, ends_ref,
    bred_ref, scaled_ref, sums_ref,
    whole_ref, side_ref, edge_ref, pair_ref,
):
    at_odd_col = odd_col()
    lane = iota((2 * ROWS, COLS), 1)
    eighth = (lane & 31) // 4
    for group in range(GROUPS):
        left = jnp.where(at_odd_col, got_one[group], got_two[group])
        right = jnp.where(at_odd_col, got_two[group], got_one[group])
        for u in range(8):
            t = group * 8 + u
            if t >= STRIPS:
                break
            strip = jnp.concatenate([own_ref[t], strip_ref[t]], axis=0)
            strip = jnp.where(eighth == 0, roll(left, 4 - 4 * u, 1), strip)
            whole_ref[t] = jnp.where(eighth == 7, roll(right, 28 - 4 * u, 1), strip)
    side_ref[:, OWN + 2 * PLANES :] = jnp.zeros((2, COLS - OWN - 2 * PLANES, COLS), F32)
    results = []
    for level in range(L):
        mixed_back = whole_ref[2 * PLANES + level]
        back = []
        for c in range(3):
            spread_back = mixed_back
            for kk in range(4):
                if kk != c:
                    spread_back = jnp.where(
                        lane // 32 == kk, roll(mixed_back, 32 * (kk - c), 1), spread_back
                    )
            back.append(spread_back[None])
        start = [
            whole_ref[2 * (c * L + level) : 2 * (c * L + level) + 2] for c in range(3)
        ]
        results.append(advance(start, back))
    for level in range(L):
        for c in range(3):
            for half in range(2):
                put_rows(side_ref, half, c * L + level, results[level][c][half])

    across = [side_ref[half].T for half in range(2)]
    lines = []
    for k in range(K):
        turned, at = across[k // 4], 32 * (k % 4)
        lines += [turned[at + 3 : at + 7], turned[at + 25 : at + 29]]
    put_table(edge_ref, 0, jnp.concatenate(lines, axis=0))
    lane = iota((OWN, COLS), 1)
    for pair in range(0, K, 2):
        fields = []
        for k in (pair, pair + 1):
            side, kk = side_ref[k // 4, 0:OWN], k % 4
            field = jnp.where(lane < 3, roll(side, -(32 * kk + 4), 1), rows_ref[k, 0:OWN])
            fields.append(jnp.where(lane >= COLS - 3, roll(side, 100 - 32 * kk, 1), field))
        for k, field in zip((pair, pair + 1), fields):
            bred_ref[k * PLANES : (k + 1) * PLANES] = field.reshape(PLANES, ROWS, COLS)

    for i in range(K):
        mine = bred_ref[i * PLANES : (i + 1) * PLANES]
        for j in range(i, K):
            other = mine if i == j else bred_ref[j * PLANES : (j + 1) * PLANES]
            row = jnp.sum(jnp.sum(mine * other, axis=0), axis=0, keepdims=True)
            pair_ref[i * K + j : i * K + j + 1] = row
            if i != j:
                pair_ref[j * K + i : j * K + i + 1] = row
    pair_ref[K * K :] = jnp.zeros((COLS - K * K, COLS), F32)
    contract_last = (((1,), (1,)), ((), ()))
    gram_row = lax.dot_general(
        jnp.ones((8, COLS), F32), pair_ref[...], contract_last,
        precision=highest, preferred_element_type=F32,
    )[0:1]

    def sample(step, carry):
        at, high2, low2 = picked(pick_ref, step)
        ends = mixed(edge_ref[...], high2, low2)
        out = part_ref[:, at]
        sub = iota((K, CHUNK), 0)
        for k in range(K):
            part = ends[k * ROWS : (k + 1) * ROWS] * ends_ref[:, at]
            out = jnp.where(sub == k, out + jnp.sum(part, axis=0, keepdims=True), out)
        scaled_ref[:, at] = out
        return carry

    lax.fori_loop(0, OBS // CHUNK, sample, 0, unroll=True)

    scaled = scaled_ref[...]
    normal = lax.dot_general(
        scaled, scaled, contract_last, precision=highest, preferred_element_type=F32
    )
    row = gram_row
    wide = jnp.concatenate([normal, jnp.zeros((K, COLS - K), F32)], axis=1)
    for i in range(K):
        row = row + roll(wide[i : i + 1], K * K + K * i, 1)
    sums_ref[...] = row


def inverse_of_factor(a):
    n = len(a)
    low = [[None] * n for _ in range(n)]
    inv = [[None] * n for _ in range(n)]
    for j in range(n):
        total = a[j][j]
        for k in range(j):
            total = total - low[j][k] * low[j][k]
        root = jnp.sqrt(total)
        inv[j][j] = 1.0 / root
        for i in range(j + 1, n):
            total = a[i][j]
            for k in range(j):
                total = total - low[i][k] * low[j][k]
            low[i][j] = total * inv[j][j]
    for j in range(n):
        for i in range(j + 1, n):
            total = low[i][j] * inv[j][j]
            for k in range(j + 1, i):
                total = total + low[i][k] * inv[k][j]
            inv[i][j] = -total * inv[i][i]
    return inv


def added(terms):
    total = terms[0]
    for term in terms[1:]:
        total = total + term
    return total


def final_kernel(cells_all, obs_all, sums_ref, bred_ref, scaled_ref, analysis_ref, perturb_ref):
    row = sums_ref[...]
    tile = (ROWS, COLS)

    def entry(at):
        return jnp.broadcast_to(row[:, at : at + 1], tile)

    gram = [[entry(i * K + j) / cells_all if j <= i else None for j in range(K)] for i in range(K)]
    normal = [[None] * K for _ in range(K)]
    for i in range(K):
        for j in range(i + 1):
            normal[i][j] = normal[j][i] = entry(K * K + i * K + j) / obs_all
    inv_lower = inverse_of_factor(gram)
    half = [
        [added([inv_lower[i][k] * normal[k][j] for k in range(i + 1)]) for j in range(K)]
        for i in range(K)
    ]
    system = [
        [
            added([half[i][k] * inv_lower[j][k] for k in range(j + 1)]) + (1.0 if i == j else 0.0)
            for j in range(i + 1)
        ]
        for i in range(K)
    ]
    inv_factor = inverse_of_factor(system)
    combo = [
        [added([inv_factor[i][k] * inv_lower[k][j] for k in range(j, i + 1)]) for j in range(i + 1)]
        for i in range(K)
    ]
    for plane in range(PLANES):
        fields = [bred_ref[j * PLANES + plane] for j in range(K)]
        for k in range(K):
            analysis_ref[k * PLANES + plane] = added(
                [combo[k][j] * fields[j] for j in range(k + 1)]
            )
    sub = iota(tile, 0)
    columns = []
    for j in range(K):
        column = jnp.zeros(tile, F32)
        for k in range(j, K):
            column = jnp.where(sub == k, combo[k][j], column)
        columns.append(column)
    for at in range(0, OBS, COLS):
        part = scaled_ref[:, at : at + COLS]
        perturb_ref[:, at : at + COLS] = added(
            [columns[j] * part[j : j + 1] for j in range(K)]
        )


def shape(*dims):
    return jax.ShapeDtypeStruct(dims, F32)


def swap(packed, axes):
    count = lax.axis_size(axes)
    first = [(i, i ^ 1) for i in range(count)]
    second = [((i - 1) % count, ((i ^ 1) - 1) % count) for i in range(count)]
    far = lax.ppermute(packed[1], axes, second)
    near = lax.ppermute(packed[0], axes, first)
    return near, far


def small(mib):
    return pltpu.CompilerParams(vmem_limit_bytes=mib << 20)


def spread(row, axes):
    count = lax.axis_size(axes)
    copies = jnp.broadcast_to(row[None], (count, 1, COLS))
    return lax.all_to_all(copies, axes, 0, 0, tiled=True).sum(axis=0)


def main_call(*operands):
    return pl.pallas_call(
        main_kernel,
        out_shape=(shape(K * PLANES, ROWS, COLS), shape(K, OBS), shape(1, COLS)),
        scratch_shapes=[
            pltpu.VMEM((STRIPS, 2 * ROWS, COLS), F32),
            pltpu.VMEM((2, COLS, COLS), F32),
            pltpu.VMEM((K * ROWS, 2 * COLS), jnp.bfloat16),
            pltpu.VMEM((COLS, COLS), F32),
        ],
        compiler_params=small(16),
        name="edges",
    )(*operands)


def busy(us):
    return pl.CostEstimate(flops=us * 10**9, bytes_accessed=0, transcendentals=0)


def local(vectors, background, obs_site, obs_offset, obs_error):
    devices_all = lax.axis_size(GX) * lax.axis_size(GY)
    cells_all = float(PLANES * ROWS * COLS * devices_all)
    obs_all = float(OBS * devices_all)
    vec = vectors.reshape(K * PLANES, ROWS, COLS)
    back = background.reshape(PLANES, ROWS, COLS)
    own = jnp.concatenate([vec, back], axis=0)
    packed = pl.pallas_call(
        pack_rows_kernel,
        out_shape=(shape(HALF, ROWS, COLS),) * 2,
        compiler_params=small(8),
        name="pack_rows",
    )(own)
    got = swap(packed, GX)
    weights = pl.pallas_call(
        weights_kernel,
        out_shape=(
            jax.ShapeDtypeStruct((2 * COLS, OBS), jnp.bfloat16),
            shape(COLS, OBS), shape(ROWS, OBS),
            shape(STRIPS, ROWS, COLS),
        ),
        compiler_params=small(8),
        cost_estimate=busy(3),
        name="weights",
    )(obs_site.reshape(1, OBS), obs_offset, obs_error.reshape(1, OBS), own)
    ext, *packed = pl.pallas_call(
        pack_cols_kernel,
        out_shape=(shape(FIELDS, 2 * ROWS, COLS),) + (shape(GROUPS, 2 * ROWS, COLS),) * 2,
        compiler_params=small(8),
        name="pack_cols",
    )(own, *got)
    got = swap(packed, GY)
    pick, weight, ends, own_strips = weights
    mine = pl.pallas_call(
        inner_kernel,
        out_shape=(shape(K, COLS, COLS), shape(STRIPS, ROWS, COLS), shape(K, OBS)),
        scratch_shapes=[pltpu.VMEM((K * COLS, 2 * COLS), jnp.bfloat16)],
        compiler_params=small(16),
        cost_estimate=busy(8),
        name="inner",
    )(ext, pick, weight)
    bred, scaled, sums = main_call(own_strips, *mine, *got, pick, ends)
    sums = spread(spread(sums, FLAT), DEEP)
    analysis, perturb = pl.pallas_call(
        functools.partial(final_kernel, cells_all, obs_all),
        out_shape=(shape(K * PLANES, ROWS, COLS), shape(K, OBS)),
        compiler_params=small(8),
        name="combine",
    )(sums, bred, scaled)
    return (analysis.reshape(vectors.shape), perturb)


def solution(mesh):
    torus = Mesh(mesh.devices.reshape(8, 4, 2, 4, 2), GX_GY)
    return jax.shard_map(
        local,
        mesh=torus,
        in_specs=(
            P(None, None, None, GX, GY),
            P(None, None, GX, GY),
            P(GX_GY),
            P(None, GX_GY),
            P(GX_GY),
        ),
        out_specs=(P(None, None, None, GX, GY), P(None, GX_GY)),
        check_vma=False,
    )
```

```python
import functools

import jax
import jax.numpy as jnp
from jax import lax
from jax.experimental import pallas as pl
from jax.experimental.pallas import tpu as pltpu
from jax.sharding import Mesh
from jax.sharding import PartitionSpec as P

K = 8
L = 4
PLANES = 3 * L
ROWS = 8
COLS = 128
OBS = 4096
GX = ("z_lo", "y")
GY = ("z_hi", "x", "core")
GX_GY = GX + GY
FLAT = ("y", "x", "core")
DEEP = ("z_lo", "z_hi")
FIELDS = K * PLANES + PLANES
HALF = FIELDS // 2
GROUPS = 4
STRIPS = 2 * PLANES + L
CHUNK = 512
BATCH = 4
OWN = PLANES * ROWS
STEP = 0.35
F32 = jnp.float32
highest = lax.Precision.HIGHEST


def iota(shape, dim):
    return lax.broadcasted_iota(jnp.int32, shape, dim)


def roll(x, shift, axis):
    axis = axis % x.ndim
    shift = shift % x.shape[axis]
    return x if shift == 0 else pltpu.roll(x, shift, axis)


def odd_row():
    return lax.rem(lax.axis_index("y"), 2) == 1


def odd_col():
    return lax.axis_index("core") == 1


def pack_rows_kernel(own_ref, one_ref, two_ref):
    odd = odd_row()
    first = own_ref[0:HALF]
    second = roll(own_ref[HALF:FIELDS], 4, 1)
    top = iota((HALF, ROWS, COLS), 1) < 4
    down = jnp.where(top, first, second)
    up = jnp.where(top, second, first)
    one_ref[...] = jnp.where(odd, down, up)
    two_ref[...] = jnp.where(odd, up, down)


def pack_cols_kernel(own_ref, got_one, got_two, ext_ref, one_ref, two_ref):
    at_odd_row = odd_row()
    at_odd_col = odd_col()
    ext_ref[:, 0:ROWS] = own_ref[...]
    top = iota((HALF, ROWS, COLS), 1) < 4
    low = jnp.where(at_odd_row, got_one[...], got_two[...])
    high = jnp.where(at_odd_row, got_two[...], got_one[...])
    ext_ref[0:HALF, ROWS : 2 * ROWS] = jnp.where(top, high, low)
    ext_ref[HALF:FIELDS, ROWS : 2 * ROWS] = roll(jnp.where(top, low, high), 4, 1)
    lane = iota((2 * ROWS, COLS), 1)
    for group in range(GROUPS):
        up = jnp.zeros((2 * ROWS, COLS), F32)
        down = jnp.zeros((2 * ROWS, COLS), F32)
        for u in range(min(8, STRIPS - group * 8)):
            for kk, field in enumerate(strip_fields(group * 8 + u)):
                moved = roll(ext_ref[field], 32 * kk + 4 * u, 1)
                down = jnp.where(lane // 4 == 8 * kk + u, moved, down)
                up = jnp.where(lane // 4 == (8 * kk + u + 31) % 32, moved, up)
        one_ref[group] = jnp.where(at_odd_col, down, up)
        two_ref[group] = jnp.where(at_odd_col, up, down)


def strip_fields(t):
    if t < 2 * PLANES:
        plane, half = t // 2, t % 2
        return [(half * 4 + kk) * PLANES + plane for kk in range(4)]
    return [K * PLANES + c * L + t - 2 * PLANES for c in range(3)]


def tendency(state, back):
    wind_x, wind_y, vort = back
    east, north, height = state

    def along_x(f):
        return 0.5 * (roll(f, -1, f.ndim - 2) - roll(f, 1, f.ndim - 2))

    def along_y(f):
        return 0.5 * (roll(f, -1, f.ndim - 1) - roll(f, 1, f.ndim - 1))

    ex, nx, hx = along_x(east), along_x(north), along_x(height)
    ey, ny, hy = along_y(east), along_y(north), along_y(height)
    tend_east = -(wind_x * ex + wind_y * ey) - hx + vort * north
    tend_north = -(wind_x * nx + wind_y * ny) - hy - vort * east
    tend_height = -(wind_x * hx + wind_y * hy) - (ex + ny)
    return tend_east, tend_north, tend_height


def advance(start, back):
    one = [s + STEP * t for s, t in zip(start, tendency(start, back))]
    two = [
        0.75 * s + 0.25 * (o + STEP * t) for s, o, t in zip(start, one, tendency(one, back))
    ]
    return [
        s / 3.0 + 2.0 / 3.0 * (w + STEP * t) for s, w, t in zip(start, two, tendency(two, back))
    ]


def put_rows(ref, k, plane, field):
    ref[k, plane * ROWS : (plane + 1) * ROWS] = field[:ROWS]
    ref[k, OWN + plane : OWN + plane + 1] = field[2 * ROWS - 1 :]
    ref[k, OWN + PLANES + plane : OWN + PLANES + plane + 1] = field[ROWS : ROWS + 1]


def put_strips(strip_ref, tile_of):
    lane = iota((ROWS, COLS), 1)
    for t in range(STRIPS):
        strip = jnp.zeros((ROWS, COLS), F32)
        for kk, field in enumerate(strip_fields(t)):
            tile = tile_of(field)
            strip = jnp.where(lane >= 32 * kk + 4, roll(tile, 32 * kk + 4, 1), strip)
            strip = jnp.where(lane >= 32 * kk + 16, roll(tile, 32 * kk + 28, 1), strip)
        strip_ref[t] = strip


def inner_kernel(ext_ref, pick_ref, weight_ref, rows_ref, strip_ref, part_ref, table_ref):
    put_strips(strip_ref, lambda field: ext_ref[field, ROWS : 2 * ROWS])
    rows_ref[:, OWN + 2 * PLANES :] = jnp.zeros((K, COLS - OWN - 2 * PLANES, COLS), F32)
    for level in range(L):
        base = K * PLANES + level
        back = [ext_ref[base + c * L][None] for c in range(3)]

        def body(i, carry, level=level, back=back):
            start = [
                jnp.stack(
                    [ext_ref[(i * BATCH + b) * PLANES + c * L + level] for b in range(BATCH)]
                )
                for c in range(3)
            ]
            done = advance(start, back)
            for c in range(3):
                for b in range(BATCH):
                    put_rows(rows_ref, i * BATCH + b, c * L + level, done[c][b])
            return carry

        lax.fori_loop(0, K // BATCH, body, 0, unroll=True)
    inner = iota((COLS, COLS), 1)
    inner = (inner >= 3) & (inner < COLS - 3)
    for k in range(K):
        put_table(table_ref, k * COLS, jnp.where(inner, rows_ref[k], 0.0).T)

    def sample(step, carry):
        at, high2, low2 = picked(pick_ref, step)
        weight = weight_ref[:, at]
        out = jnp.zeros((K, CHUNK), F32)
        sub = iota((K, CHUNK), 0)
        for k in range(K):
            part = mixed(table_ref[k * COLS : (k + 1) * COLS], high2, low2) * weight
            out = jnp.where(sub == k, jnp.sum(part, axis=0, keepdims=True), out)
        part_ref[:, at] = out
        return carry

    lax.fori_loop(0, OBS // CHUNK, sample, 0, unroll=True)


def picked(pick_ref, step):
    at = pl.ds(pl.multiple_of(step * CHUNK, CHUNK), CHUNK)
    high, low = pick_ref[0:COLS, at], pick_ref[COLS : 2 * COLS, at]
    return at, jnp.concatenate([high, high], axis=0), jnp.concatenate([low, low], axis=0)


def mixed(part, high2, low2):
    return jnp.dot(part, high2, preferred_element_type=F32) + jnp.dot(
        part, low2, preferred_element_type=F32
    )


def put_table(ref, at, value):
    high = value.astype(jnp.bfloat16)
    low = (value - high.astype(F32)).astype(jnp.bfloat16)
    ref[at : at + value.shape[0], 0:COLS] = high
    ref[at : at + value.shape[0], COLS : 2 * COLS] = low


def weights_kernel(
    site_ref, off_ref, err_ref, own_ref, pick_ref, weight_ref, ends_ref, strip_ref
):
    put_strips(strip_ref, lambda field: own_ref[field])

    def step(i, carry):
        at = pl.ds(pl.multiple_of(i * CHUNK, CHUNK), CHUNK)
        site = site_ref[:, at]
        shift_x = off_ref[0:1, at]
        shift_y = off_ref[1:2, at]
        row_at = site // COLS
        plane = site // (ROWS * COLS)
        row = row_at % ROWS
        col = site % COLS
        size_x = jnp.abs(shift_x)
        size_y = jnp.abs(shift_y)
        before = jnp.where(row == 0, OWN + plane, row_at - 1)
        after = jnp.where(row == ROWS - 1, OWN + PLANES + plane, row_at + 1)
        beside = jnp.where(shift_x < 0.0, before, after)
        next_col = jnp.where(shift_y < 0.0, col - 1, col + 1)
        own_x = 1.0 - size_x
        scale = 1.0 / jnp.sqrt(err_ref[:, at])
        own_y = (1.0 - size_y) * scale
        side_y = size_y * scale

        def split(value):
            high = value.astype(jnp.bfloat16).astype(F32)
            return high, value - high

        own_high, own_low = split(own_x)
        side_high, side_low = split(size_x)
        index = iota((COLS, CHUNK), 0)
        at_own = index == row_at
        at_side = index == beside
        pick_high = jnp.where(at_own, own_high, jnp.where(at_side, side_high, 0.0))
        pick_low = jnp.where(at_own, own_low, jnp.where(at_side, side_low, 0.0))
        pick_ref[0:COLS, at] = pick_high.astype(jnp.bfloat16)
        pick_ref[COLS : 2 * COLS, at] = pick_low.astype(jnp.bfloat16)
        weight_ref[:, at] = jnp.where(
            index == col, own_y, jnp.where(index == next_col, side_y, 0.0)
        )
        line = iota((ROWS, CHUNK), 0)
        line = jnp.where(line < 4, line - 1, line + COLS - 7)
        ends_ref[:, at] = jnp.where(line == col, own_y, jnp.where(line == next_col, side_y, 0.0))
        return carry

    lax.fori_loop(0, OBS // CHUNK, step, 0)


def main_kernel(
    own_ref, rows_ref, strip_ref, part_ref, got_one, got_two, pick_ref, ends_ref,
    bred_ref, scaled_ref, sums_ref,
    whole_ref, side_ref, edge_ref, pair_ref,
):
    at_odd_col = odd_col()
    lane = iota((2 * ROWS, COLS), 1)
    eighth = (lane & 31) // 4
    for group in range(GROUPS):
        left = jnp.where(at_odd_col, got_one[group], got_two[group])
        right = jnp.where(at_odd_col, got_two[group], got_one[group])
        for u in range(8):
            t = group * 8 + u
            if t >= STRIPS:
                break
            strip = jnp.concatenate([own_ref[t], strip_ref[t]], axis=0)
            strip = jnp.where(eighth == 0, roll(left, 4 - 4 * u, 1), strip)
            whole_ref[t] = jnp.where(eighth == 7, roll(right, 28 - 4 * u, 1), strip)
    side_ref[:, OWN + 2 * PLANES :] = jnp.zeros((2, COLS - OWN - 2 * PLANES, COLS), F32)
    results = []
    for level in range(L):
        mixed_back = whole_ref[2 * PLANES + level]
        back = []
        for c in range(3):
            spread_back = mixed_back
            for kk in range(4):
                if kk != c:
                    spread_back = jnp.where(
                        lane // 32 == kk, roll(mixed_back, 32 * (kk - c), 1), spread_back
                    )
            back.append(spread_back[None])
        start = [
            whole_ref[2 * (c * L + level) : 2 * (c * L + level) + 2] for c in range(3)
        ]
        results.append(advance(start, back))
    for level in range(L):
        for c in range(3):
            for half in range(2):
                put_rows(side_ref, half, c * L + level, results[level][c][half])

    across = [side_ref[half].T for half in range(2)]
    lines = []
    for k in range(K):
        turned, at = across[k // 4], 32 * (k % 4)
        lines += [turned[at + 3 : at + 7], turned[at + 25 : at + 29]]
    put_table(edge_ref, 0, jnp.concatenate(lines, axis=0))
    lane = iota((OWN, COLS), 1)
    for pair in range(0, K, 2):
        fields = []
        for k in (pair, pair + 1):
            side, kk = side_ref[k // 4, 0:OWN], k % 4
            field = jnp.where(lane < 3, roll(side, -(32 * kk + 4), 1), rows_ref[k, 0:OWN])
            fields.append(jnp.where(lane >= COLS - 3, roll(side, 100 - 32 * kk, 1), field))
        for k, field in zip((pair, pair + 1), fields):
            bred_ref[k * PLANES : (k + 1) * PLANES] = field.reshape(PLANES, ROWS, COLS)

    for i in range(K):
        mine = bred_ref[i * PLANES : (i + 1) * PLANES]
        for j in range(i, K):
            other = mine if i == j else bred_ref[j * PLANES : (j + 1) * PLANES]
            row = jnp.sum(jnp.sum(mine * other, axis=0), axis=0, keepdims=True)
            pair_ref[i * K + j : i * K + j + 1] = row
            if i != j:
                pair_ref[j * K + i : j * K + i + 1] = row
    pair_ref[K * K :] = jnp.zeros((COLS - K * K, COLS), F32)
    contract_last = (((1,), (1,)), ((), ()))
    gram_row = lax.dot_general(
        jnp.ones((8, COLS), F32), pair_ref[...], contract_last,
        precision=highest, preferred_element_type=F32,
    )[0:1]

    def sample(step, carry):
        at, high2, low2 = picked(pick_ref, step)
        ends = mixed(edge_ref[...], high2, low2)
        out = part_ref[:, at]
        sub = iota((K, CHUNK), 0)
        for k in range(K):
            part = ends[k * ROWS : (k + 1) * ROWS] * ends_ref[:, at]
            out = jnp.where(sub == k, out + jnp.sum(part, axis=0, keepdims=True), out)
        scaled_ref[:, at] = out
        return carry

    lax.fori_loop(0, OBS // CHUNK, sample, 0, unroll=True)

    scaled = scaled_ref[...]
    normal = lax.dot_general(
        scaled, scaled, contract_last, precision=highest, preferred_element_type=F32
    )
    row = gram_row
    wide = jnp.concatenate([normal, jnp.zeros((K, COLS - K), F32)], axis=1)
    for i in range(K):
        row = row + roll(wide[i : i + 1], K * K + K * i, 1)
    sums_ref[...] = row


def inverse_of_factor(a):
    n = len(a)
    low = [[None] * n for _ in range(n)]
    inv = [[None] * n for _ in range(n)]
    for j in range(n):
        total = a[j][j]
        for k in range(j):
            total = total - low[j][k] * low[j][k]
        guess = lax.rsqrt(total)
        inv[j][j] = guess * (1.5 - 0.5 * (total * guess) * guess)
        for i in range(j + 1, n):
            total = a[i][j]
            for k in range(j):
                total = total - low[i][k] * low[j][k]
            low[i][j] = total * inv[j][j]
    for j in range(n):
        for i in range(j + 1, n):
            total = low[i][j] * inv[j][j]
            for k in range(j + 1, i):
                total = total + low[i][k] * inv[k][j]
            inv[i][j] = -total * inv[i][i]
    return inv


def added(terms):
    total = terms[0]
    for term in terms[1:]:
        total = total + term
    return total


def final_kernel(cells_all, obs_all, sums_ref, bred_ref, scaled_ref, analysis_ref, perturb_ref):
    row = sums_ref[...]
    tile = (ROWS, COLS)

    def entry(at):
        return jnp.broadcast_to(row[:, at : at + 1], tile)

    gram = [[entry(i * K + j) / cells_all if j <= i else None for j in range(K)] for i in range(K)]
    normal = [[None] * K for _ in range(K)]
    for i in range(K):
        for j in range(i + 1):
            normal[i][j] = normal[j][i] = entry(K * K + i * K + j) / obs_all
    inv_lower = inverse_of_factor(gram)
    half = [
        [added([inv_lower[i][k] * normal[k][j] for k in range(i + 1)]) for j in range(K)]
        for i in range(K)
    ]
    system = [
        [
            added([half[i][k] * inv_lower[j][k] for k in range(j + 1)]) + (1.0 if i == j else 0.0)
            for j in range(i + 1)
        ]
        for i in range(K)
    ]
    inv_factor = inverse_of_factor(system)
    combo = [
        [added([inv_factor[i][k] * inv_lower[k][j] for k in range(j, i + 1)]) for j in range(i + 1)]
        for i in range(K)
    ]
    for plane in range(PLANES):
        fields = [bred_ref[j * PLANES + plane] for j in range(K)]
        for k in range(K):
            analysis_ref[k * PLANES + plane] = added(
                [combo[k][j] * fields[j] for j in range(k + 1)]
            )
    sub = iota(tile, 0)
    columns = []
    for j in range(K):
        column = jnp.zeros(tile, F32)
        for k in range(j, K):
            column = jnp.where(sub == k, combo[k][j], column)
        columns.append(column)
    for at in range(0, OBS, COLS):
        part = scaled_ref[:, at : at + COLS]
        perturb_ref[:, at : at + COLS] = added(
            [columns[j] * part[j : j + 1] for j in range(K)]
        )


def shape(*dims):
    return jax.ShapeDtypeStruct(dims, F32)


def swap(packed, axes):
    count = lax.axis_size(axes)
    first = [(i, i ^ 1) for i in range(count)]
    second = [((i - 1) % count, ((i ^ 1) - 1) % count) for i in range(count)]
    far = lax.ppermute(packed[1], axes, second)
    near = lax.ppermute(packed[0], axes, first)
    return near, far


def small(mib):
    return pltpu.CompilerParams(vmem_limit_bytes=mib << 20)


def spread(row, axes):
    count = lax.axis_size(axes)
    copies = jnp.broadcast_to(row[None], (count, 1, COLS))
    return lax.all_to_all(copies, axes, 0, 0, tiled=True).sum(axis=0)


def main_call(*operands):
    return pl.pallas_call(
        main_kernel,
        out_shape=(shape(K * PLANES, ROWS, COLS), shape(K, OBS), shape(1, COLS)),
        scratch_shapes=[
            pltpu.VMEM((STRIPS, 2 * ROWS, COLS), F32),
            pltpu.VMEM((2, COLS, COLS), F32),
            pltpu.VMEM((K * ROWS, 2 * COLS), jnp.bfloat16),
            pltpu.VMEM((COLS, COLS), F32),
        ],
        compiler_params=small(16),
        name="edges",
    )(*operands)


def busy(us):
    return pl.CostEstimate(flops=us * 10**9, bytes_accessed=0, transcendentals=0)


def local(vectors, background, obs_site, obs_offset, obs_error):
    devices_all = lax.axis_size(GX) * lax.axis_size(GY)
    cells_all = float(PLANES * ROWS * COLS * devices_all)
    obs_all = float(OBS * devices_all)
    vec = vectors.reshape(K * PLANES, ROWS, COLS)
    back = background.reshape(PLANES, ROWS, COLS)
    own = jnp.concatenate([vec, back], axis=0)
    packed = pl.pallas_call(
        pack_rows_kernel,
        out_shape=(shape(HALF, ROWS, COLS),) * 2,
        compiler_params=small(8),
        name="pack_rows",
    )(own)
    got = swap(packed, GX)
    weights = pl.pallas_call(
        weights_kernel,
        out_shape=(
            jax.ShapeDtypeStruct((2 * COLS, OBS), jnp.bfloat16),
            shape(COLS, OBS), shape(ROWS, OBS),
            shape(STRIPS, ROWS, COLS),
        ),
        compiler_params=small(8),
        cost_estimate=busy(3),
        name="weights",
    )(obs_site.reshape(1, OBS), obs_offset, obs_error.reshape(1, OBS), own)
    ext, *packed = pl.pallas_call(
        pack_cols_kernel,
        out_shape=(shape(FIELDS, 2 * ROWS, COLS),) + (shape(GROUPS, 2 * ROWS, COLS),) * 2,
        compiler_params=small(8),
        name="pack_cols",
    )(own, *got)
    got = swap(packed, GY)
    pick, weight, ends, own_strips = weights
    mine = pl.pallas_call(
        inner_kernel,
        out_shape=(shape(K, COLS, COLS), shape(STRIPS, ROWS, COLS), shape(K, OBS)),
        scratch_shapes=[pltpu.VMEM((K * COLS, 2 * COLS), jnp.bfloat16)],
        compiler_params=small(16),
        cost_estimate=busy(8),
        name="inner",
    )(ext, pick, weight)
    bred, scaled, sums = main_call(own_strips, *mine, *got, pick, ends)
    sums = spread(spread(sums, DEEP), FLAT)
    analysis, perturb = pl.pallas_call(
        functools.partial(final_kernel, cells_all, obs_all),
        out_shape=(shape(K * PLANES, ROWS, COLS), shape(K, OBS)),
        compiler_params=small(8),
        name="combine",
    )(sums, bred, scaled)
    return (analysis.reshape(vectors.shape), perturb)


def solution(mesh):
    torus = Mesh(mesh.devices.reshape(8, 4, 2, 4, 2), GX_GY)
    return jax.shard_map(
        local,
        mesh=torus,
        in_specs=(
            P(None, None, None, GX, GY),
            P(None, None, GX, GY),
            P(GX_GY),
            P(None, GX_GY),
            P(GX_GY),
        ),
        out_specs=(P(None, None, None, GX, GY), P(None, GX_GY)),
        check_vma=False,
    )
```

```python
import functools

import jax
import jax.numpy as jnp
from jax import lax
from jax.experimental import pallas as pl
from jax.experimental.pallas import tpu as pltpu
from jax.sharding import Mesh
from jax.sharding import PartitionSpec as P

K = 8
L = 4
PLANES = 3 * L
ROWS = 8
COLS = 128
OBS = 4096
GX = ("z_lo", "y")
GY = ("z_hi", "x", "core")
GX_GY = GX + GY
FLAT = ("y", "x", "core")
DEEP = ("z_lo", "z_hi")
FIELDS = K * PLANES + PLANES
HALF = FIELDS // 2
GROUPS = 4
STRIPS = 2 * PLANES + L
CHUNK = 512
BATCH = 4
OWN = PLANES * ROWS
STEP = 0.35
F32 = jnp.float32
highest = lax.Precision.HIGHEST


def iota(shape, dim):
    return lax.broadcasted_iota(jnp.int32, shape, dim)


def roll(x, shift, axis):
    axis = axis % x.ndim
    shift = shift % x.shape[axis]
    return x if shift == 0 else pltpu.roll(x, shift, axis)


def odd_row():
    return lax.rem(lax.axis_index("y"), 2) == 1


def odd_col():
    return lax.axis_index("core") == 1


def pack_rows_kernel(own_ref, one_ref, two_ref):
    odd = odd_row()
    first = own_ref[0:HALF]
    second = roll(own_ref[HALF:FIELDS], 4, 1)
    top = iota((HALF, ROWS, COLS), 1) < 4
    down = jnp.where(top, first, second)
    up = jnp.where(top, second, first)
    one_ref[...] = jnp.where(odd, down, up)
    two_ref[...] = jnp.where(odd, up, down)


def pack_cols_kernel(own_ref, got_one, got_two, ext_ref, one_ref, two_ref):
    at_odd_row = odd_row()
    at_odd_col = odd_col()
    ext_ref[:, 0:ROWS] = own_ref[...]
    top = iota((HALF, ROWS, COLS), 1) < 4
    low = jnp.where(at_odd_row, got_one[...], got_two[...])
    high = jnp.where(at_odd_row, got_two[...], got_one[...])
    ext_ref[0:HALF, ROWS : 2 * ROWS] = jnp.where(top, high, low)
    ext_ref[HALF:FIELDS, ROWS : 2 * ROWS] = roll(jnp.where(top, low, high), 4, 1)
    lane = iota((2 * ROWS, COLS), 1)
    for group in range(GROUPS):
        up = jnp.zeros((2 * ROWS, COLS), F32)
        down = jnp.zeros((2 * ROWS, COLS), F32)
        for u in range(min(8, STRIPS - group * 8)):
            for kk, field in enumerate(strip_fields(group * 8 + u)):
                moved = roll(ext_ref[field], 32 * kk + 4 * u, 1)
                down = jnp.where(lane // 4 == 8 * kk + u, moved, down)
                up = jnp.where(lane // 4 == (8 * kk + u + 31) % 32, moved, up)
        one, two = jnp.where(at_odd_col, down, up), jnp.where(at_odd_col, up, down)
        at = 2 * group
        if group < GROUPS - 1:
            for ref, tile in ((one_ref, one), (two_ref, two)):
                ref[at] = tile[:ROWS]
                ref[at + 1] = tile[ROWS:]
        else:
            eighth = (iota((ROWS, COLS), 1) & 31) // 4
            below = eighth < 4
            above = (eighth < 3) | (eighth == 7)
            down = jnp.where(below, down[:ROWS], roll(down[ROWS:], 16, 1))
            up = jnp.where(above, up[:ROWS], roll(up[ROWS:], 16, 1))
            one_ref[at] = jnp.where(at_odd_col, down, up)
            two_ref[at] = jnp.where(at_odd_col, up, down)


def received(ref, group):
    first = ref[2 * group]
    second = ref[2 * group + 1] if group < GROUPS - 1 else roll(first, -16, 1)
    return jnp.concatenate([first, second], axis=0)


def strip_fields(t):
    if t < 2 * PLANES:
        plane, half = t // 2, t % 2
        return [(half * 4 + kk) * PLANES + plane for kk in range(4)]
    return [K * PLANES + c * L + t - 2 * PLANES for c in range(3)]


def tendency(state, back):
    wind_x, wind_y, vort = back
    east, north, height = state

    def along_x(f):
        return 0.5 * (roll(f, -1, f.ndim - 2) - roll(f, 1, f.ndim - 2))

    def along_y(f):
        return 0.5 * (roll(f, -1, f.ndim - 1) - roll(f, 1, f.ndim - 1))

    ex, nx, hx = along_x(east), along_x(north), along_x(height)
    ey, ny, hy = along_y(east), along_y(north), along_y(height)
    tend_east = -(wind_x * ex + wind_y * ey) - hx + vort * north
    tend_north = -(wind_x * nx + wind_y * ny) - hy - vort * east
    tend_height = -(wind_x * hx + wind_y * hy) - (ex + ny)
    return tend_east, tend_north, tend_height


def advance(start, back):
    one = [s + STEP * t for s, t in zip(start, tendency(start, back))]
    two = [
        0.75 * s + 0.25 * (o + STEP * t) for s, o, t in zip(start, one, tendency(one, back))
    ]
    return [
        s / 3.0 + 2.0 / 3.0 * (w + STEP * t) for s, w, t in zip(start, two, tendency(two, back))
    ]


def put_rows(ref, k, plane, field):
    ref[k, plane * ROWS : (plane + 1) * ROWS] = field[:ROWS]
    ref[k, OWN + plane : OWN + plane + 1] = field[2 * ROWS - 1 :]
    ref[k, OWN + PLANES + plane : OWN + PLANES + plane + 1] = field[ROWS : ROWS + 1]


def put_strips(strip_ref, tile_of):
    lane = iota((ROWS, COLS), 1)
    for t in range(STRIPS):
        strip = jnp.zeros((ROWS, COLS), F32)
        for kk, field in enumerate(strip_fields(t)):
            tile = tile_of(field)
            strip = jnp.where(lane >= 32 * kk + 4, roll(tile, 32 * kk + 4, 1), strip)
            strip = jnp.where(lane >= 32 * kk + 16, roll(tile, 32 * kk + 28, 1), strip)
        strip_ref[t] = strip


def inner_kernel(ext_ref, pick_ref, weight_ref, rows_ref, strip_ref, part_ref, table_ref):
    put_strips(strip_ref, lambda field: ext_ref[field, ROWS : 2 * ROWS])
    rows_ref[:, OWN + 2 * PLANES :] = jnp.zeros((K, COLS - OWN - 2 * PLANES, COLS), F32)
    for level in range(L):
        base = K * PLANES + level
        back = [ext_ref[base + c * L][None] for c in range(3)]

        def body(i, carry, level=level, back=back):
            start = [
                jnp.stack(
                    [ext_ref[(i * BATCH + b) * PLANES + c * L + level] for b in range(BATCH)]
                )
                for c in range(3)
            ]
            done = advance(start, back)
            for c in range(3):
                for b in range(BATCH):
                    put_rows(rows_ref, i * BATCH + b, c * L + level, done[c][b])
            return carry

        lax.fori_loop(0, K // BATCH, body, 0, unroll=True)
    inner = iota((COLS, COLS), 1)
    inner = (inner >= 3) & (inner < COLS - 3)
    for k in range(K):
        put_table(table_ref, k * COLS, jnp.where(inner, rows_ref[k], 0.0).T)

    def sample(step, carry):
        at, high2, low2 = picked(pick_ref, step)
        weight = weight_ref[:, at]
        out = jnp.zeros((K, CHUNK), F32)
        sub = iota((K, CHUNK), 0)
        for k in range(K):
            part = mixed(table_ref[k * COLS : (k + 1) * COLS], high2, low2) * weight
            out = jnp.where(sub == k, jnp.sum(part, axis=0, keepdims=True), out)
        part_ref[:, at] = out
        return carry

    lax.fori_loop(0, OBS // CHUNK, sample, 0, unroll=True)


def picked(pick_ref, step):
    at = pl.ds(pl.multiple_of(step * CHUNK, CHUNK), CHUNK)
    high, low = pick_ref[0:COLS, at], pick_ref[COLS : 2 * COLS, at]
    return at, jnp.concatenate([high, high], axis=0), jnp.concatenate([low, low], axis=0)


def mixed(part, high2, low2):
    return jnp.dot(part, high2, preferred_element_type=F32) + jnp.dot(
        part, low2, preferred_element_type=F32
    )


def put_table(ref, at, value):
    high = value.astype(jnp.bfloat16)
    low = (value - high.astype(F32)).astype(jnp.bfloat16)
    ref[at : at + value.shape[0], 0:COLS] = high
    ref[at : at + value.shape[0], COLS : 2 * COLS] = low


def weights_kernel(
    site_ref, off_ref, err_ref, own_ref, pick_ref, weight_ref, ends_ref, strip_ref
):
    put_strips(strip_ref, lambda field: own_ref[field])

    def step(i, carry):
        at = pl.ds(pl.multiple_of(i * CHUNK, CHUNK), CHUNK)
        site = site_ref[:, at]
        shift_x = off_ref[0:1, at]
        shift_y = off_ref[1:2, at]
        row_at = site // COLS
        plane = site // (ROWS * COLS)
        row = row_at % ROWS
        col = site % COLS
        size_x = jnp.abs(shift_x)
        size_y = jnp.abs(shift_y)
        before = jnp.where(row == 0, OWN + plane, row_at - 1)
        after = jnp.where(row == ROWS - 1, OWN + PLANES + plane, row_at + 1)
        beside = jnp.where(shift_x < 0.0, before, after)
        next_col = jnp.where(shift_y < 0.0, col - 1, col + 1)
        own_x = 1.0 - size_x
        scale = 1.0 / jnp.sqrt(err_ref[:, at])
        own_y = (1.0 - size_y) * scale
        side_y = size_y * scale

        def split(value):
            high = value.astype(jnp.bfloat16).astype(F32)
            return high, value - high

        own_high, own_low = split(own_x)
        side_high, side_low = split(size_x)
        index = iota((COLS, CHUNK), 0)
        at_own = index == row_at
        at_side = index == beside
        pick_high = jnp.where(at_own, own_high, jnp.where(at_side, side_high, 0.0))
        pick_low = jnp.where(at_own, own_low, jnp.where(at_side, side_low, 0.0))
        pick_ref[0:COLS, at] = pick_high.astype(jnp.bfloat16)
        pick_ref[COLS : 2 * COLS, at] = pick_low.astype(jnp.bfloat16)
        weight_ref[:, at] = jnp.where(
            index == col, own_y, jnp.where(index == next_col, side_y, 0.0)
        )
        line = iota((ROWS, CHUNK), 0)
        line = jnp.where(line < 4, line - 1, line + COLS - 7)
        ends_ref[:, at] = jnp.where(line == col, own_y, jnp.where(line == next_col, side_y, 0.0))
        return carry

    lax.fori_loop(0, OBS // CHUNK, step, 0)


def main_kernel(
    own_ref, rows_ref, strip_ref, part_ref, got_one, got_two, pick_ref, ends_ref,
    bred_ref, scaled_ref, sums_ref,
    whole_ref, side_ref, edge_ref, pair_ref,
):
    at_odd_col = odd_col()
    lane = iota((2 * ROWS, COLS), 1)
    eighth = (lane & 31) // 4
    for group in range(GROUPS):
        one, two = received(got_one, group), received(got_two, group)
        left = jnp.where(at_odd_col, one, two)
        right = jnp.where(at_odd_col, two, one)
        for u in range(8):
            t = group * 8 + u
            if t >= STRIPS:
                break
            strip = jnp.concatenate([own_ref[t], strip_ref[t]], axis=0)
            strip = jnp.where(eighth == 0, roll(left, 4 - 4 * u, 1), strip)
            whole_ref[t] = jnp.where(eighth == 7, roll(right, 28 - 4 * u, 1), strip)
    side_ref[:, OWN + 2 * PLANES :] = jnp.zeros((2, COLS - OWN - 2 * PLANES, COLS), F32)
    results = []
    for level in range(L):
        mixed_back = whole_ref[2 * PLANES + level]
        back = []
        for c in range(3):
            spread_back = mixed_back
            for kk in range(4):
                if kk != c:
                    spread_back = jnp.where(
                        lane // 32 == kk, roll(mixed_back, 32 * (kk - c), 1), spread_back
                    )
            back.append(spread_back[None])
        start = [
            whole_ref[2 * (c * L + level) : 2 * (c * L + level) + 2] for c in range(3)
        ]
        results.append(advance(start, back))
    for level in range(L):
        for c in range(3):
            for half in range(2):
                put_rows(side_ref, half, c * L + level, results[level][c][half])

    across = [side_ref[half].T for half in range(2)]
    lines = []
    for k in range(K):
        turned, at = across[k // 4], 32 * (k % 4)
        lines += [turned[at + 3 : at + 7], turned[at + 25 : at + 29]]
    put_table(edge_ref, 0, jnp.concatenate(lines, axis=0))
    lane = iota((OWN, COLS), 1)
    for pair in range(0, K, 2):
        fields = []
        for k in (pair, pair + 1):
            side, kk = side_ref[k // 4, 0:OWN], k % 4
            field = jnp.where(lane < 3, roll(side, -(32 * kk + 4), 1), rows_ref[k, 0:OWN])
            fields.append(jnp.where(lane >= COLS - 3, roll(side, 100 - 32 * kk, 1), field))
        for k, field in zip((pair, pair + 1), fields):
            bred_ref[k * PLANES : (k + 1) * PLANES] = field.reshape(PLANES, ROWS, COLS)

    for i in range(K):
        mine = bred_ref[i * PLANES : (i + 1) * PLANES]
        for j in range(i, K):
            other = mine if i == j else bred_ref[j * PLANES : (j + 1) * PLANES]
            row = jnp.sum(jnp.sum(mine * other, axis=0), axis=0, keepdims=True)
            pair_ref[i * K + j : i * K + j + 1] = row
            if i != j:
                pair_ref[j * K + i : j * K + i + 1] = row
    pair_ref[K * K :] = jnp.zeros((COLS - K * K, COLS), F32)
    contract_last = (((1,), (1,)), ((), ()))
    gram_row = lax.dot_general(
        jnp.ones((8, COLS), F32), pair_ref[...], contract_last,
        precision=highest, preferred_element_type=F32,
    )[0:1]

    def sample(step, carry):
        at, high2, low2 = picked(pick_ref, step)
        ends = mixed(edge_ref[...], high2, low2)
        out = part_ref[:, at]
        sub = iota((K, CHUNK), 0)
        for k in range(K):
            part = ends[k * ROWS : (k + 1) * ROWS] * ends_ref[:, at]
            out = jnp.where(sub == k, out + jnp.sum(part, axis=0, keepdims=True), out)
        scaled_ref[:, at] = out
        return carry

    lax.fori_loop(0, OBS // CHUNK, sample, 0, unroll=True)

    scaled = scaled_ref[...]
    normal = lax.dot_general(
        scaled, scaled, contract_last, precision=highest, preferred_element_type=F32
    )
    row = gram_row
    wide = jnp.concatenate([normal, jnp.zeros((K, COLS - K), F32)], axis=1)
    for i in range(K):
        row = row + roll(wide[i : i + 1], K * K + K * i, 1)
    sums_ref[...] = row


def inverse_of_factor(a):
    n = len(a)
    low = [[None] * n for _ in range(n)]
    inv = [[None] * n for _ in range(n)]
    for j in range(n):
        total = a[j][j]
        for k in range(j):
            total = total - low[j][k] * low[j][k]
        root = jnp.sqrt(total)
        inv[j][j] = 1.0 / root
        for i in range(j + 1, n):
            total = a[i][j]
            for k in range(j):
                total = total - low[i][k] * low[j][k]
            low[i][j] = total * inv[j][j]
    for j in range(n):
        for i in range(j + 1, n):
            total = low[i][j] * inv[j][j]
            for k in range(j + 1, i):
                total = total + low[i][k] * inv[k][j]
            inv[i][j] = -total * inv[i][i]
    return inv


def added(terms):
    total = terms[0]
    for term in terms[1:]:
        total = total + term
    return total


def final_kernel(cells_all, obs_all, sums_ref, bred_ref, scaled_ref, analysis_ref, perturb_ref):
    row = sums_ref[...]
    tile = (ROWS, COLS)

    def entry(at):
        return jnp.broadcast_to(row[:, at : at + 1], tile)

    gram = [[entry(i * K + j) / cells_all if j <= i else None for j in range(K)] for i in range(K)]
    normal = [[None] * K for _ in range(K)]
    for i in range(K):
        for j in range(i + 1):
            normal[i][j] = normal[j][i] = entry(K * K + i * K + j) / obs_all
    inv_lower = inverse_of_factor(gram)
    half = [
        [added([inv_lower[i][k] * normal[k][j] for k in range(i + 1)]) for j in range(K)]
        for i in range(K)
    ]
    system = [
        [
            added([half[i][k] * inv_lower[j][k] for k in range(j + 1)]) + (1.0 if i == j else 0.0)
            for j in range(i + 1)
        ]
        for i in range(K)
    ]
    inv_factor = inverse_of_factor(system)
    combo = [
        [added([inv_factor[i][k] * inv_lower[k][j] for k in range(j, i + 1)]) for j in range(i + 1)]
        for i in range(K)
    ]
    for plane in range(PLANES):
        fields = [bred_ref[j * PLANES + plane] for j in range(K)]
        for k in range(K):
            analysis_ref[k * PLANES + plane] = added(
                [combo[k][j] * fields[j] for j in range(k + 1)]
            )
    sub = iota(tile, 0)
    columns = []
    for j in range(K):
        column = jnp.zeros(tile, F32)
        for k in range(j, K):
            column = jnp.where(sub == k, combo[k][j], column)
        columns.append(column)
    for at in range(0, OBS, COLS):
        part = scaled_ref[:, at : at + COLS]
        perturb_ref[:, at : at + COLS] = added(
            [columns[j] * part[j : j + 1] for j in range(K)]
        )


def shape(*dims):
    return jax.ShapeDtypeStruct(dims, F32)


def swap(packed, axes):
    count = lax.axis_size(axes)
    first = [(i, i ^ 1) for i in range(count)]
    second = [((i - 1) % count, ((i ^ 1) - 1) % count) for i in range(count)]
    far = lax.ppermute(packed[1], axes, second)
    near = lax.ppermute(packed[0], axes, first)
    return near, far


def small(mib):
    return pltpu.CompilerParams(vmem_limit_bytes=mib << 20)


def spread(row, axes):
    count = lax.axis_size(axes)
    copies = jnp.broadcast_to(row[None], (count, 1, COLS))
    return lax.all_to_all(copies, axes, 0, 0, tiled=True).sum(axis=0)


def main_call(*operands):
    return pl.pallas_call(
        main_kernel,
        out_shape=(shape(K * PLANES, ROWS, COLS), shape(K, OBS), shape(1, COLS)),
        scratch_shapes=[
            pltpu.VMEM((STRIPS, 2 * ROWS, COLS), F32),
            pltpu.VMEM((2, COLS, COLS), F32),
            pltpu.VMEM((K * ROWS, 2 * COLS), jnp.bfloat16),
            pltpu.VMEM((COLS, COLS), F32),
        ],
        compiler_params=small(16),
        name="edges",
    )(*operands)


def busy(us):
    return pl.CostEstimate(flops=us * 10**9, bytes_accessed=0, transcendentals=0)


def local(vectors, background, obs_site, obs_offset, obs_error):
    devices_all = lax.axis_size(GX) * lax.axis_size(GY)
    cells_all = float(PLANES * ROWS * COLS * devices_all)
    obs_all = float(OBS * devices_all)
    vec = vectors.reshape(K * PLANES, ROWS, COLS)
    back = background.reshape(PLANES, ROWS, COLS)
    own = jnp.concatenate([vec, back], axis=0)
    packed = pl.pallas_call(
        pack_rows_kernel,
        out_shape=(shape(HALF, ROWS, COLS),) * 2,
        compiler_params=small(8),
        name="pack_rows",
    )(own)
    got = swap(packed, GX)
    weights = pl.pallas_call(
        weights_kernel,
        out_shape=(
            jax.ShapeDtypeStruct((2 * COLS, OBS), jnp.bfloat16),
            shape(COLS, OBS), shape(ROWS, OBS),
            shape(STRIPS, ROWS, COLS),
        ),
        compiler_params=small(8),
        cost_estimate=busy(3),
        name="weights",
    )(obs_site.reshape(1, OBS), obs_offset, obs_error.reshape(1, OBS), own)
    ext, *packed = pl.pallas_call(
        pack_cols_kernel,
        out_shape=(shape(FIELDS, 2 * ROWS, COLS),) + (shape(2 * GROUPS - 1, ROWS, COLS),) * 2,
        compiler_params=small(8),
        name="pack_cols",
    )(own, *got)
    got = swap(packed, GY)
    pick, weight, ends, own_strips = weights
    mine = pl.pallas_call(
        inner_kernel,
        out_shape=(shape(K, COLS, COLS), shape(STRIPS, ROWS, COLS), shape(K, OBS)),
        scratch_shapes=[pltpu.VMEM((K * COLS, 2 * COLS), jnp.bfloat16)],
        compiler_params=small(16),
        cost_estimate=busy(8),
        name="inner",
    )(ext, pick, weight)
    bred, scaled, sums = main_call(own_strips, *mine, *got, pick, ends)
    sums = spread(spread(sums, FLAT), DEEP)
    analysis, perturb = pl.pallas_call(
        functools.partial(final_kernel, cells_all, obs_all),
        out_shape=(shape(K * PLANES, ROWS, COLS), shape(K, OBS)),
        compiler_params=small(8),
        name="combine",
    )(sums, bred, scaled)
    return (analysis.reshape(vectors.shape), perturb)


def solution(mesh):
    torus = Mesh(mesh.devices.reshape(8, 4, 2, 4, 2), GX_GY)
    return jax.shard_map(
        local,
        mesh=torus,
        in_specs=(
            P(None, None, None, GX, GY),
            P(None, None, GX, GY),
            P(GX_GY),
            P(None, GX_GY),
            P(GX_GY),
        ),
        out_specs=(P(None, None, None, GX, GY), P(None, GX_GY)),
        check_vma=False,
    )
```
